256 devices in a mesh: chan: 32 (over z_lo, x, core), inp: 8 (over z_hi, y).
Axes of the slice: x: 4, y: 4, z: 8 (z_hi: 2, z_lo: 4; z = z_hi * 4 + z_lo), core: 2. Of those that a mesh axis runs over, the one named last changes fastest.
Arguments:
- voltages: bfloat16 [512, 2, 131072], P('inp', None, 'chan'), may hold values from -64 to 64
Outputs:
- delays: float32 [512, 512, 2, 512], P('inp', 'chan')
The draws below stay inside these ranges and needn't reach their ends.
All inputs are finite; a program needn't handle non-finite values.
Results may differ from the reference program's by a relative error of at most 0.0053.
Values may be sent and summed in bfloat16 or wider, within the bound.
No kernel may reach another device: no remote copies, remote signals or barrier semaphores. Data moves between devices by JAX's collectives and lax.ppermute only.
A program may use at most 128 MiB of HBM per device.

```python
import math
import jax
import jax.numpy as jnp
from jax import lax

NINP = 512
NCH = 512
NSPEC = 256
TIME = 131072
N_INP = 8


def draw_voltages(key, part):
    subkeys = jax.random.split(key, 6)
    input_gains = jnp.exp(jax.random.uniform(subkeys[0], (NINP,), jnp.float32, math.log(0.5), math.log(4.0)))
    noise_part = jax.random.normal(subkeys[1], (NINP, 2, TIME), jnp.float32)
    amplitude = jax.random.uniform(subkeys[5], (NINP,), jnp.float32, 0.1, 0.4)
    fir_taps = 0.5 * jax.random.normal(subkeys[2], (NINP, 3), jnp.float32)
    colored = noise_part
    for offset in range(3):
        colored = colored + fir_taps[:, offset, None, None] * jnp.roll(noise_part, offset + 1, axis=2)
    sky_signal = jax.random.normal(subkeys[3], (2, TIME), jnp.float32)
    shifts = jnp.stack([jnp.roll(sky_signal, offset, axis=1) for offset in range(8)])
    delay_steps = jax.random.randint(subkeys[4], (NINP,), 0, 8)
    onehot = (delay_steps[:, None] == jnp.arange(8)[None, :]).astype(jnp.float32)
    delayed = jnp.einsum('im,mpt->ipt', onehot, shifts)
    voltage_draw = input_gains[:, None, None] * (colored + amplitude[:, None, None] * delayed)
    return jnp.clip(voltage_draw, -64.0, 64.0).astype(jnp.bfloat16)


def setup_inputs(seed: int = 0) -> dict:
    keys = jax.random.split(jax.random.key(seed), 2)
    voltages = draw_voltages(jax.random.fold_in(keys[1], 71), 0)
    return dict(voltages=voltages)


def taper_weights(count):
    position = jnp.arange(count, dtype=jnp.float32)
    return 0.5 - 0.5 * jnp.cos(2.0 * math.pi * (position + 0.5) / count)

def channel_table(count):
    indices = jnp.arange(count, dtype=jnp.int32)
    product = indices[:, None] * indices[None, :] % count
    angle = 2.0 * math.pi / count * product.astype(jnp.float32)
    window = taper_weights(count)[:, None] / math.sqrt(count)
    cosine = window * jnp.cos(angle)
    sine = window * jnp.sin(angle)
    upper = jnp.concatenate([cosine, -sine], axis=1)
    lower = jnp.concatenate([sine, cosine], axis=1)
    return jnp.concatenate([upper, lower], axis=0).astype(jnp.bfloat16)

def round_half(values):
    narrow = lax.optimization_barrier(values.astype(jnp.bfloat16))
    return narrow.astype(jnp.float32)

def reference(voltages):
    block_rows = NINP // N_INP
    samples = voltages.reshape(NINP, 2, NSPEC, NCH).transpose(0, 2, 1, 3).reshape(NINP * NSPEC, 2 * NCH)
    spectra = jnp.dot(samples, channel_table(NCH), preferred_element_type=jnp.float32).astype(jnp.bfloat16)
    spectra = spectra.reshape(NINP, NSPEC, 2, NCH)
    stacked = spectra.transpose(3, 0, 2, 1).reshape(NCH, NINP, 2 * NSPEC).astype(jnp.float32)
    rotated = jnp.concatenate([-stacked[:, :, NSPEC:], stacked[:, :, :NSPEC]], axis=2)
    power = lax.optimization_barrier(jnp.sum(stacked * stacked, axis=2)) / NSPEC + 1e-06
    inverse_root = lax.rsqrt(power)
    taper = taper_weights(NCH)
    factor = math.sqrt(NSPEC / NCH)

    def one_block(block_index):
        start = (block_index * block_rows).astype(jnp.int32)
        rows = lax.dynamic_slice_in_dim(stacked, start, block_rows, 1)
        real_part = jnp.einsum('cit,cjt->cij', rows, stacked, precision=lax.Precision.HIGHEST)
        imag_part = jnp.einsum('cit,cjt->cij', rows, rotated, precision=lax.Precision.HIGHEST)
        row_scale = lax.dynamic_slice_in_dim(inverse_root, start, block_rows, 1)
        scaling = row_scale[:, :, None] * inverse_root[:, None, :] / NSPEC
        rho_real = round_half(real_part * scaling) * taper[:, None, None]
        rho_imag = round_half(imag_part * scaling) * taper[:, None, None]
        complex_vis = rho_real + 1j * rho_imag
        spectrum = jnp.fft.fft(complex_vis, axis=0) * factor
        result = jnp.stack([jnp.real(spectrum), jnp.imag(spectrum)], axis=0).transpose(2, 3, 0, 1)
        rows_global = start + jnp.arange(block_rows, dtype=jnp.int32)
        cols_global = jnp.arange(NINP, dtype=jnp.int32)
        same = rows_global[:, None] == cols_global[None, :]
        return jnp.where(same[:, :, None, None], jnp.zeros_like(result), result)
    blocks = lax.map(one_block, jnp.arange(N_INP, dtype=jnp.int32))
    return blocks.reshape(NINP, NINP, 2, NCH)
```

```python
import functools
import math

import jax
import jax.numpy as jnp
import ml_dtypes
import numpy as np
from jax import lax
from jax.experimental import pallas as pl
from jax.experimental.pallas import tpu as pltpu
from jax.sharding import PartitionSpec as P

NCH = 512
NSPEC = 256
LANES = 128
ALL = ("inp", "chan")


def taper_weights(count):
    position = np.arange(count, dtype=np.float64)
    return 0.5 - 0.5 * np.cos(2.0 * np.pi * (position + 0.5) / count)


def channel_tables():
    index = np.arange(NCH)
    angle = 2.0 * np.pi / NCH * (index[:, None] * index[None, :] % NCH)
    window = taper_weights(NCH)[None, :] / math.sqrt(NCH)
    cosine = (window * np.cos(angle)).astype(np.float32).astype(ml_dtypes.bfloat16)
    sine = (window * np.sin(angle)).astype(np.float32).astype(ml_dtypes.bfloat16)
    return cosine, sine


def delay_tables():
    channel = np.arange(NCH)
    half = NCH // 2
    angle = 2.0 * np.pi / NCH * (channel[:, None] * np.arange(half)[None, :] % NCH)
    weight = taper_weights(NCH)[:, None] * math.sqrt(NSPEC / NCH)
    both = np.concatenate([weight * np.cos(angle), weight * np.sin(angle)], axis=1)
    both = both.reshape(half, 2, NCH).transpose(1, 0, 2)
    return both.astype(np.float32).astype(ml_dtypes.bfloat16)


def channelize_kernel(volt_ref, cos_ref, sin_ref, out_ref, wide_ref, *, rows, spec_local):
    contract = (((1,), (1,)), ((), ()))
    for pair in range(spec_local // 2):
        plain, turned = [], []
        for spec in (2 * pair, 2 * pair + 1):
            real = volt_ref[0, :, spec * NCH : (spec + 1) * NCH]
            imag = volt_ref[1, :, spec * NCH : (spec + 1) * NCH]
            plain += [real, imag]
            turned += [imag, -real]
        plain = jnp.concatenate(plain, axis=0)
        turned = jnp.concatenate(turned, axis=0)
        out = lax.dot_general(cos_ref[...], plain, contract, preferred_element_type=jnp.float32)
        out += lax.dot_general(sin_ref[...], turned, contract, preferred_element_type=jnp.float32)
        for k in range(2):
            wide_ref[pl.ds(2 * pair + k, NCH, stride=spec_local), :] = out[:, k * LANES : (k + 1) * LANES]
    out_ref[...] = wide_ref[...].astype(jnp.bfloat16)


def correlate_kernel(spec_ref, out_ref, x_ref, scale_ref, *, blocks, times, rows):
    half = LANES // 2
    lane = lax.broadcasted_iota(jnp.int32, (rows, LANES), 1)
    row = lax.broadcasted_iota(jnp.int32, (rows, LANES), 0)
    sign = jnp.where(lane < half, 1.0, -1.0)
    diagonal = (lane % half) == row
    for ch in range(2):
        for block in range(blocks):
            part = spec_ref[block * times : (block + 1) * times, ch * 8 : (ch + 1) * 8, :]
            part = part.astype(jnp.float32).reshape(times * 8, LANES)
            x_ref[ch, :, block * LANES : (block + 1) * LANES] = part.astype(jnp.bfloat16)
            total = jnp.sum(part * part, axis=0, keepdims=True)
            total = total + pltpu.roll(total, half, axis=1)
            scale_ref[ch, block : block + 1, :] = lax.rsqrt(total / NSPEC + 1e-06)

    contract = (((0,), (0,)), ((), ()))
    for ch in range(2):
        for jblock in range(blocks):
            left = x_ref[ch, :, jblock * LANES : (jblock + 1) * LANES]
            product = lax.dot_general(left, x_ref[ch], contract, preferred_element_type=jnp.float32)
            row_scale = scale_ref[ch, jblock : jblock + 1, :]
            row_scale = jnp.transpose(jnp.broadcast_to(row_scale, (LANES, LANES)))[:rows] / NSPEC
            for iblock in range(blocks):
                first = product[:rows, iblock * LANES : (iblock + 1) * LANES]
                second = product[rows:, iblock * LANES : (iblock + 1) * LANES]
                value = first + sign * pltpu.roll(second, half, axis=1)
                value = value * (row_scale * scale_ref[ch, iblock : iblock + 1, :])
                if iblock == jblock:
                    value = jnp.where(diagonal, 0.0, value)
                value = value.astype(jnp.bfloat16)
                for a in range(4):
                    out_ref[iblock, jblock, a, ch] = value[a * 16 : (a + 1) * 16]


def delay_kernel(rho_ref, table_ref, out_ref, wide_ref, *, owners, rows, cols):
    half = NCH // 2
    wide_ref[...] = rho_ref[...].astype(jnp.float32)
    contract = (((0,), (0,)), ((), ()))
    group = 4
    for first in range(0, cols, group):
        parts = []
        for ch in range(2):
            left = [
                wide_ref[pl.ds(ch * cols + first + g, owners, stride=2 * cols), :].astype(jnp.bfloat16)
                for g in range(group)
            ]
            left = jnp.concatenate(left, axis=1)
            parts.append(
                lax.dot_general(left, table_ref[ch], contract, preferred_element_type=jnp.float32)
            )
        for g in range(group):
            sums = []
            for product in parts:
                real = product[g * LANES : g * LANES + rows]
                imag = product[g * LANES + rows : (g + 1) * LANES]
                sums.append((real[:, :half] + imag[:, half:], imag[:, :half] - real[:, half:]))
            even, odd = sums
            for part in range(2):
                low = even[part] + odd[part]
                high = even[part] - odd[part]
                for kb, value in enumerate((low[:, :LANES], low[:, LANES:], high[:, :LANES], high[:, LANES:])):
                    start = (first + g) * 8 + kb * 2 + part
                    out_ref[pl.ds(start, rows, stride=cols * 8), :] = value


def vmem(shape, dtype):
    return pltpu.VMEM(shape, dtype)


def shards(voltages):
    rows, _, local_time = voltages.shape
    chan_count = lax.axis_size("chan")
    inp_count = lax.axis_size("inp")
    owners = chan_count * inp_count
    spec_local = local_time // NCH
    cols = rows * inp_count // chan_count
    cosine, sine = channel_tables()
    slab = 2 * spec_local
    whole = pl.BlockSpec(memory_space=pltpu.VMEM)

    planes = voltages.transpose(1, 0, 2)
    spectra = pl.pallas_call(
        functools.partial(channelize_kernel, rows=rows, spec_local=spec_local),
        out_shape=jax.ShapeDtypeStruct((NCH * spec_local, LANES), jnp.bfloat16),
        in_specs=[whole] * 3,
        out_specs=whole,
        scratch_shapes=[vmem((NCH * spec_local, LANES), jnp.float32)],
        name="channelize",
    )(planes, jnp.asarray(cosine), jnp.asarray(sine))

    turned = lax.all_to_all(spectra.reshape(owners, slab, LANES), ALL, 0, 0, tiled=True)

    rho = pl.pallas_call(
        functools.partial(correlate_kernel, blocks=inp_count, times=chan_count, rows=rows),
        out_shape=jax.ShapeDtypeStruct((inp_count, inp_count, 4, 2, cols, LANES), jnp.bfloat16),
        in_specs=[whole],
        out_specs=whole,
        scratch_shapes=[
            vmem((2, NSPEC, inp_count * LANES), jnp.bfloat16),
            vmem((2, inp_count, LANES), jnp.float32),
        ],
        name="correlate",
    )(turned)

    rho = lax.all_to_all(rho.reshape(owners, 2 * cols, LANES), ALL, 0, 0, tiled=True)

    out = pl.pallas_call(
        functools.partial(delay_kernel, owners=owners, rows=rows, cols=cols),
        out_shape=jax.ShapeDtypeStruct((rows * cols * 8, LANES), jnp.float32),
        in_specs=[whole] * 2,
        out_specs=whole,
        scratch_shapes=[vmem((owners * 2 * cols, LANES), jnp.float32)],
        name="delay",
    )(rho.reshape(owners * 2 * cols, LANES), jnp.asarray(delay_tables()))
    out = out.reshape(rows, cols, NCH // LANES, 2, LANES).transpose(0, 1, 3, 2, 4)
    return out.reshape(rows, cols, 2, NCH)


def solution(mesh):
    return jax.shard_map(
        shards,
        mesh=mesh,
        in_specs=(P("inp", None, "chan"),),
        out_specs=P("inp", "chan", None, None),
        check_vma=False,
    )
```

```python
import functools
import math

import jax
import jax.numpy as jnp
import ml_dtypes
import numpy as np
from jax import lax
from jax.experimental import pallas as pl
from jax.experimental.pallas import tpu as pltpu
from jax.sharding import PartitionSpec as P

NCH = 512
NSPEC = 256
LANES = 128
ALL = ("inp", "chan")


def taper_weights(count):
    position = np.arange(count, dtype=np.float64)
    return 0.5 - 0.5 * np.cos(2.0 * np.pi * (position + 0.5) / count)


def channel_tables():
    index = np.arange(NCH)
    angle = 2.0 * np.pi / NCH * (index[:, None] * index[None, :] % NCH)
    window = taper_weights(NCH)[None, :] / math.sqrt(NCH)
    cosine = (window * np.cos(angle)).astype(np.float32).astype(ml_dtypes.bfloat16)
    sine = (window * np.sin(angle)).astype(np.float32).astype(ml_dtypes.bfloat16)
    return cosine, sine


def delay_tables():
    channel = np.arange(NCH)
    half = NCH // 2
    angle = 2.0 * np.pi / NCH * (channel[:, None] * np.arange(half)[None, :] % NCH)
    weight = taper_weights(NCH)[:, None] * math.sqrt(NSPEC / NCH)
    both = np.concatenate([weight * np.cos(angle), weight * np.sin(angle)], axis=1)
    both = both.reshape(half, 2, NCH).transpose(1, 0, 2)
    return both.astype(np.float32).astype(ml_dtypes.bfloat16)


def channelize_kernel(volt_ref, cos_ref, sin_ref, out_ref, wide_ref, *, rows, spec_local):
    contract = (((1,), (1,)), ((), ()))
    for pair in range(spec_local // 2):
        plain, turned = [], []
        for spec in (2 * pair, 2 * pair + 1):
            real = volt_ref[0, :, spec * NCH : (spec + 1) * NCH]
            imag = volt_ref[1, :, spec * NCH : (spec + 1) * NCH]
            plain += [real, imag]
            turned += [imag, -real]
        plain = jnp.concatenate(plain, axis=0)
        turned = jnp.concatenate(turned, axis=0)
        out = lax.dot_general(cos_ref[...], plain, contract, preferred_element_type=jnp.float32)
        out += lax.dot_general(sin_ref[...], turned, contract, preferred_element_type=jnp.float32)
        for k in range(2):
            wide_ref[pl.ds(2 * pair + k, NCH, stride=spec_local), :] = out[:, k * LANES : (k + 1) * LANES]
    out_ref[...] = wide_ref[...].astype(jnp.bfloat16)


def correlate_kernel(
    spec_ref, out_ref, left_ref, right_ref, row_ref, col_ref, stage_ref, sems, *, blocks, times, rows
):
    half = LANES // 2
    lane = lax.broadcasted_iota(jnp.int32, (1, LANES), 1)
    sign = jnp.where(lane < half, 1.0, -1.0)
    for ch in range(2):
        for block in range(blocks):
            part = spec_ref[block * times : (block + 1) * times, ch * 8 : (ch + 1) * 8, :]
            part = part.astype(jnp.float32).reshape(times * 8, LANES)
            span = slice(block * LANES, (block + 1) * LANES)
            right_ref[ch, :NSPEC, span] = part.astype(jnp.bfloat16)
            right_ref[ch, NSPEC:, span] = (pltpu.roll(part, half, axis=1) * sign).astype(jnp.bfloat16)
            flipped = jnp.transpose(part.astype(jnp.bfloat16))
            left_ref[ch, block * rows : (block + 1) * rows, :NSPEC] = flipped[:rows]
            left_ref[ch, block * rows : (block + 1) * rows, NSPEC:] = flipped[rows:]
            total = jnp.sum(part * part, axis=0, keepdims=True)
            total = total + pltpu.roll(total, half, axis=1)
            scale = lax.rsqrt(total / NSPEC + 1e-06)
            col_ref[ch, block : block + 1, :] = scale
            scale = jnp.transpose(jnp.broadcast_to(scale, (LANES, LANES)))[:rows] / NSPEC
            row_ref[ch, block * rows : (block + 1) * rows, :] = scale

    diagonal = lax.broadcasted_iota(jnp.int32, (rows, LANES), 1) % half == lax.broadcasted_iota(
        jnp.int32, (rows, LANES), 0
    )
    copies = []
    for ch in range(2):
        for pair in range(blocks // 2):
            product = jnp.dot(
                left_ref[ch],
                right_ref[ch, :, pair * 2 * LANES : (pair + 1) * 2 * LANES],
                preferred_element_type=jnp.float32,
            )
            for iblock in (2 * pair, 2 * pair + 1):
                col = col_ref[ch, iblock : iblock + 1, :]
                for jblock in range(blocks):
                    span = slice(jblock * rows, (jblock + 1) * rows)
                    value = product[span, (iblock % 2) * LANES : (iblock % 2 + 1) * LANES]
                    value = value * (row_ref[ch, span, :] * col)
                    if iblock == jblock:
                        value = jnp.where(diagonal, 0.0, value)
                    value = value.astype(jnp.bfloat16)
                    for a in range(4):
                        stage_ref[ch, iblock, jblock, a] = value[a * 16 : (a + 1) * 16]
                copy = pltpu.make_async_copy(
                    stage_ref.at[ch, iblock], out_ref.at[iblock, :, :, ch], sems.at[ch, iblock]
                )
                copy.start()
                copies.append(copy)
    for copy in copies:
        copy.wait()


def delay_kernel(rho_ref, table_ref, out_ref, wide_ref, stage_ref, sems, *, owners, rows, cols):
    half = NCH // 2
    contract = (((0,), (0,)), ((), ()))
    group = 4
    sections = 2 * cols // 8
    flat_ref = stage_ref.reshape(cols * rows * 8, LANES)
    for section in range(sections):
        part = rho_ref[:, section * 8 : (section + 1) * 8, :].astype(jnp.float32)
        wide_ref[section] = part.reshape(owners * 8, LANES)
    copies = []
    for first in range(0, cols, group):
        parts = []
        for ch in range(2):
            left = []
            for g in range(group):
                row = ch * cols + first + g
                left.append(wide_ref[row // 8, pl.ds(row % 8, owners, stride=8), :].astype(jnp.bfloat16))
            left = jnp.concatenate(left, axis=1)
            parts.append(
                lax.dot_general(left, table_ref[ch], contract, preferred_element_type=jnp.float32)
            )
        for g in range(group):
            sums = []
            for product in parts:
                real = product[g * LANES : g * LANES + rows]
                imag = product[g * LANES + rows : (g + 1) * LANES]
                sums.append((real[:, :half] + imag[:, half:], imag[:, :half] - real[:, half:]))
            even, odd = sums
            for part in range(2):
                low = even[part] + odd[part]
                high = even[part] - odd[part]
                for kb, value in enumerate((low[:, :LANES], low[:, LANES:], high[:, :LANES], high[:, LANES:])):
                    start = (first + g) * rows * 8 + kb * 2 + part
                    flat_ref[pl.ds(start, rows, stride=8), :] = value
            copy = pltpu.make_async_copy(
                stage_ref.at[first + g], out_ref.at[:, first + g], sems.at[first + g]
            )
            copy.start()
            copies.append(copy)
    for copy in copies:
        copy.wait()


def fast(array):
    return pltpu.with_memory_space_constraint(array, pltpu.VMEM)


def shards(voltages):
    rows, _, local_time = voltages.shape
    chan_count = lax.axis_size("chan")
    inp_count = lax.axis_size("inp")
    owners = chan_count * inp_count
    spec_local = local_time // NCH
    cols = rows * inp_count // chan_count
    inputs = rows * inp_count
    cosine, sine = channel_tables()
    slab = 2 * spec_local
    whole = pl.BlockSpec(memory_space=pltpu.VMEM)

    planes = voltages.transpose(1, 0, 2)
    spectra = pl.pallas_call(
        functools.partial(channelize_kernel, rows=rows, spec_local=spec_local),
        out_shape=pltpu.VMEM((NCH * spec_local, LANES), jnp.bfloat16),
        in_specs=[whole] * 3,
        out_specs=whole,
        scratch_shapes=[pltpu.VMEM((NCH * spec_local, LANES), jnp.float32)],
        name="channelize",
    )(fast(planes), fast(jnp.asarray(cosine)), fast(jnp.asarray(sine)))

    turned = lax.all_to_all(spectra.reshape(owners, slab, LANES), ALL, 0, 0, tiled=True)

    rho = pl.pallas_call(
        functools.partial(correlate_kernel, blocks=inp_count, times=chan_count, rows=rows),
        out_shape=jax.ShapeDtypeStruct((inp_count, inp_count, 4, 2, cols, LANES), jnp.bfloat16),
        in_specs=[whole],
        out_specs=pl.BlockSpec(memory_space=pl.ANY),
        scratch_shapes=[
            pltpu.VMEM((2, inputs, 2 * NSPEC), jnp.bfloat16),
            pltpu.VMEM((2, 2 * NSPEC, 2 * inputs), jnp.bfloat16),
            pltpu.VMEM((2, inputs, LANES), jnp.float32),
            pltpu.VMEM((2, inp_count, LANES), jnp.float32),
            pltpu.VMEM((2, inp_count, inp_count, 4, cols, LANES), jnp.bfloat16),
            pltpu.SemaphoreType.DMA((2, inp_count)),
        ],
        name="correlate",
    )(fast(turned))

    rho = lax.all_to_all(rho.reshape(owners, 2 * cols, LANES), ALL, 0, 0, tiled=True)

    out = pl.pallas_call(
        functools.partial(delay_kernel, owners=owners, rows=rows, cols=cols),
        out_shape=jax.ShapeDtypeStruct((rows, cols, 8, LANES), jnp.float32),
        in_specs=[whole] * 2,
        out_specs=pl.BlockSpec(memory_space=pl.ANY),
        scratch_shapes=[
            pltpu.VMEM((2 * cols // 8, owners * 8, LANES), jnp.float32),
            pltpu.VMEM((cols, rows, 8, LANES), jnp.float32),
            pltpu.SemaphoreType.DMA((cols,)),
        ],
        name="delay",
    )(fast(rho), fast(jnp.asarray(delay_tables())))
    out = out.reshape(rows, cols, NCH // LANES, 2, LANES).transpose(0, 1, 3, 2, 4)
    return out.reshape(rows, cols, 2, NCH)


def solution(mesh):
    return jax.shard_map(
        shards,
        mesh=mesh,
        in_specs=(P("inp", None, "chan"),),
        out_specs=P("inp", "chan", None, None),
        check_vma=False,
    )
```

```python
import functools
import math

import jax
import jax.numpy as jnp
import ml_dtypes
import numpy as np
from jax import lax
from jax.experimental import pallas as pl
from jax.experimental.pallas import tpu as pltpu
from jax.sharding import PartitionSpec as P

NCH = 512
NSPEC = 256
LANES = 128
ALL = ("inp", "chan")


def taper_weights(count):
    position = np.arange(count, dtype=np.float64)
    return 0.5 - 0.5 * np.cos(2.0 * np.pi * (position + 0.5) / count)


def channel_tables():
    half = NCH // 2
    index = np.arange(NCH)
    angle = 2.0 * np.pi / NCH * (np.arange(half + 16)[:, None] * index[None, :] % NCH)
    window = taper_weights(NCH)[None, :] / math.sqrt(NCH)
    cosine = window * np.cos(angle)
    cosine[half + 1 :] = 0.0
    sine = (window * np.sin(angle))[:half]
    return tuple(part.astype(np.float32).astype(ml_dtypes.bfloat16) for part in (cosine, sine))


def delay_tables():
    half = NCH // 2
    owner = np.arange(half)
    channel = np.stack([owner, np.where(owner == 0, half, NCH - owner)])
    angle = 2.0 * np.pi / NCH * (channel[:, :, None] * np.arange(half) % NCH)
    weight = taper_weights(NCH)[channel][:, :, None] * math.sqrt(NSPEC / NCH)
    both = np.concatenate([weight * np.cos(angle), weight * np.sin(angle)], axis=2)
    both = both.reshape(2, half // 2, 2, NCH).transpose(2, 0, 1, 3).reshape(2, half, NCH)
    return both.astype(np.float32).astype(ml_dtypes.bfloat16)


def channelize_kernel(
    volt_hbm, cos_hbm, sin_hbm, out_ref, raw_ref, cos_ref, sin_ref, part_ref, wide_ref, sems, *, rows, specs
):
    half = NCH // 2
    tiles = NCH // LANES
    copies = [
        pltpu.make_async_copy(cos_hbm, cos_ref, sems.at[0]),
        pltpu.make_async_copy(sin_hbm, sin_ref, sems.at[1]),
    ]
    for spec in range(specs):
        copies.append(pltpu.make_async_copy(volt_hbm.at[:, spec], raw_ref.at[spec], sems.at[2 + spec]))
    for copy in (*copies[2:6], copies[0], copies[1], *copies[6:]):
        copy.start()

    def planes(spec):
        part_ref[spec] = raw_ref[spec].astype(jnp.float32).reshape(rows * 8, LANES)
        both = []
        for part in range(2):
            pieces = [part_ref[spec, pl.ds(2 * t + part, rows, stride=8), :] for t in range(tiles)]
            both.append(jnp.concatenate(pieces, axis=1).astype(jnp.bfloat16))
        return both

    contract = (((1,), (1,)), ((), ()))
    for pair in range(specs // 2):
        plain, turned = [], []
        if pair % 2 == 0:
            for copy in copies[2 + 2 * pair : 6 + 2 * pair]:
                copy.wait()
        for spec in (2 * pair, 2 * pair + 1):
            real, imag = planes(spec)
            plain += [real, imag]
            turned += [imag, -real]
        if pair == 0:
            copies[0].wait()
            copies[1].wait()
        even = lax.dot_general(
            cos_ref[...], jnp.concatenate(plain, axis=0), contract, preferred_element_type=jnp.float32
        )
        odd = lax.dot_general(
            sin_ref[...], jnp.concatenate(turned, axis=0), contract, preferred_element_type=jnp.float32
        )
        for k in range(2):
            spec = 2 * pair + k
            span = slice(k * LANES, (k + 1) * LANES)
            wide_ref[0, pl.ds(spec, half, stride=specs), :] = even[:half, span] + odd[:, span]
            wide_ref[1, pl.ds(spec, half, stride=specs), :] = even[:half, span] - odd[:, span]
            wide_ref[1, spec : spec + 1, :] = even[half : half + 1, span]
    first = wide_ref[0].reshape(half, specs, LANES)
    second = wide_ref[1].reshape(half, specs, LANES)
    out_ref[...] = jnp.concatenate([first, second], axis=1).astype(jnp.bfloat16)


def correlate_kernel(
    spec_ref, out_ref, left_ref, right_ref, row_ref, col_ref, stage_ref, sems, *, blocks, times, rows
):
    half = LANES // 2
    lane = lax.broadcasted_iota(jnp.int32, (1, LANES), 1)
    sign = jnp.where(lane < half, 1.0, -1.0)
    diagonal = lax.broadcasted_iota(jnp.int32, (rows, LANES), 1) % half == lax.broadcasted_iota(
        jnp.int32, (rows, LANES), 0
    )
    copies = []

    def prepare(ch, block):
        part = spec_ref[block * times : (block + 1) * times, ch * 8 : (ch + 1) * 8, :]
        part = part.astype(jnp.float32).reshape(times * 8, LANES)
        narrow = part.astype(jnp.bfloat16)
        span = slice(block * LANES, (block + 1) * LANES)
        right_ref[ch, :NSPEC, span] = narrow
        right_ref[ch, NSPEC:, span] = (pltpu.roll(part, half, axis=1) * sign).astype(jnp.bfloat16)
        flipped = jnp.transpose(narrow)
        left_ref[ch, block * rows : (block + 1) * rows, :NSPEC] = flipped[:rows]
        left_ref[ch, block * rows : (block + 1) * rows, NSPEC:] = flipped[rows:]
        total = jnp.sum(part * part, axis=0, keepdims=True)
        total = total + pltpu.roll(total, half, axis=1)
        scale = lax.rsqrt(total / NSPEC + 1e-06)
        col_ref[ch, block : block + 1, :] = scale
        scale = jnp.transpose(jnp.broadcast_to(scale, (LANES, LANES)))[:rows] / NSPEC
        row_ref[ch, block * rows : (block + 1) * rows, :] = scale

    def multiply(ch, pair):
        product = jnp.dot(
            left_ref[ch],
            right_ref[ch, :, pair * 2 * LANES : (pair + 1) * 2 * LANES],
            preferred_element_type=jnp.float32,
        )
        for iblock in (2 * pair, 2 * pair + 1):
            col = col_ref[ch, iblock : iblock + 1, :]
            for jblock in range(blocks):
                span = slice(jblock * rows, (jblock + 1) * rows)
                value = product[span, (iblock % 2) * LANES : (iblock % 2 + 1) * LANES]
                value = value * (row_ref[ch, span, :] * col)
                if iblock == jblock:
                    value = jnp.where(diagonal, 0.0, value)
                value = value.astype(jnp.bfloat16)
                for a in range(4):
                    stage_ref[ch, iblock, jblock, a] = value[a * 16 : (a + 1) * 16]
            copy = pltpu.make_async_copy(
                stage_ref.at[ch, iblock], out_ref.at[iblock, :, :, ch], sems.at[ch, iblock]
            )
            copy.start()
            copies.append(copy)

    for block in range(blocks):
        prepare(0, block)
    for pair in range(blocks // 2):
        multiply(0, pair)
        prepare(1, 2 * pair)
        prepare(1, 2 * pair + 1)
    for pair in range(blocks // 2):
        multiply(1, pair)
    for copy in copies:
        copy.wait()


def delay_kernel(rho_ref, table_ref, out_ref, wide_ref, stage_ref, sems, *, owners, rows, cols):
    half = NCH // 2
    contract = (((0,), (0,)), ((), ()))
    sections = 2 * cols // 8
    flat_ref = stage_ref.reshape(cols * rows * 8, LANES)
    copies = []

    def widen(section):
        part = rho_ref[:, section * 8 : (section + 1) * 8, :].astype(jnp.float32)
        part = part.reshape(owners // 2, 2, 8, LANES)
        for parity in range(2):
            wide_ref[section, parity] = part[:, parity].reshape(owners * 4, LANES)

    def transform(first, group):
        parts = []
        for parity in range(2):
            left = []
            for col in range(first, first + group):
                pieces = []
                for ch in range(2):
                    row = ch * cols + col
                    pieces.append(wide_ref[row // 8, parity, pl.ds(row % 8, owners // 2, stride=8), :])
                left.append(jnp.concatenate(pieces, axis=0).astype(jnp.bfloat16))
            left = jnp.concatenate(left, axis=1)
            parts.append(
                lax.dot_general(left, table_ref[parity], contract, preferred_element_type=jnp.float32)
            )
        for g in range(group):
            sums = []
            for product in parts:
                real = product[g * LANES : g * LANES + rows]
                imag = product[g * LANES + rows : (g + 1) * LANES]
                sums.append((real[:, :half] + imag[:, half:], imag[:, :half] - real[:, half:]))
            even, odd = sums
            for part in range(2):
                low = even[part] + odd[part]
                high = even[part] - odd[part]
                for kb, value in enumerate((low[:, :LANES], low[:, LANES:], high[:, :LANES], high[:, LANES:])):
                    start = (first + g) * rows * 8 + kb * 2 + part
                    flat_ref[pl.ds(start, rows, stride=8), :] = value
            copy = pltpu.make_async_copy(
                stage_ref.at[first + g], out_ref.at[:, first + g], sems.at[first + g]
            )
            copy.start()
            copies.append(copy)

    group = 4
    for first in range(0, cols, group):
        if first % 8 == 0:
            for ch in range(2):
                widen((ch * cols + first) // 8)
        transform(first, group)
    for copy in copies:
        copy.wait()


def fast(array):
    return pltpu.with_memory_space_constraint(array, pltpu.VMEM)


def shards(voltages):
    rows, _, local_time = voltages.shape
    chan_count = lax.axis_size("chan")
    inp_count = lax.axis_size("inp")
    owners = chan_count * inp_count
    spec_local = local_time // NCH
    cols = rows * inp_count // chan_count
    inputs = rows * inp_count
    cosine, sine = channel_tables()
    slab = 2 * spec_local
    tiles = NCH // LANES
    whole = pl.BlockSpec(memory_space=pltpu.VMEM)
    place = pl.BlockSpec(memory_space=pl.ANY)

    rowed = voltages.reshape(rows, 2, local_time // LANES, LANES).transpose(0, 2, 1, 3)
    rowed = rowed.reshape(rows, spec_local, 2 * tiles, LANES)
    spectra = pl.pallas_call(
        functools.partial(channelize_kernel, rows=rows, specs=spec_local),
        out_shape=pltpu.VMEM((owners, slab, LANES), jnp.bfloat16),
        in_specs=[place] * 3,
        out_specs=whole,
        scratch_shapes=[
            pltpu.VMEM((spec_local, rows, 2 * tiles, LANES), jnp.bfloat16),
            pltpu.VMEM(cosine.shape, jnp.bfloat16),
            pltpu.VMEM(sine.shape, jnp.bfloat16),
            pltpu.VMEM((spec_local, rows * 2 * tiles, LANES), jnp.float32),
            pltpu.VMEM((2, NCH // 2 * spec_local, LANES), jnp.float32),
            pltpu.SemaphoreType.DMA((2 + spec_local,)),
        ],
        name="channelize",
    )(rowed, jnp.asarray(cosine), jnp.asarray(sine))

    turned = lax.all_to_all(spectra, ALL, 0, 0, tiled=True)

    rho = pl.pallas_call(
        functools.partial(correlate_kernel, blocks=inp_count, times=chan_count, rows=rows),
        out_shape=jax.ShapeDtypeStruct((inp_count, inp_count, 4, 2, cols, LANES), jnp.bfloat16),
        in_specs=[whole],
        out_specs=place,
        scratch_shapes=[
            pltpu.VMEM((2, inputs, 2 * NSPEC), jnp.bfloat16),
            pltpu.VMEM((2, 2 * NSPEC, 2 * inputs), jnp.bfloat16),
            pltpu.VMEM((2, inputs, LANES), jnp.float32),
            pltpu.VMEM((2, inp_count, LANES), jnp.float32),
            pltpu.VMEM((2, inp_count, inp_count, 4, cols, LANES), jnp.bfloat16),
            pltpu.SemaphoreType.DMA((2, inp_count)),
        ],
        name="correlate",
    )(fast(turned))

    rho = lax.all_to_all(rho.reshape(owners, 2 * cols, LANES), ALL, 0, 0, tiled=True)

    out = pl.pallas_call(
        functools.partial(delay_kernel, owners=owners, rows=rows, cols=cols),
        out_shape=jax.ShapeDtypeStruct((rows, cols, 8, LANES), jnp.float32),
        in_specs=[whole] * 2,
        out_specs=place,
        scratch_shapes=[
            pltpu.VMEM((2 * cols // 8, 2, owners * 4, LANES), jnp.float32),
            pltpu.VMEM((cols, rows, 8, LANES), jnp.float32),
            pltpu.SemaphoreType.DMA((cols,)),
        ],
        name="delay",
    )(fast(rho), fast(jnp.asarray(delay_tables())))
    out = out.reshape(rows, cols, NCH // LANES, 2, LANES).transpose(0, 1, 3, 2, 4)
    return out.reshape(rows, cols, 2, NCH)


def solution(mesh):
    return jax.shard_map(
        shards,
        mesh=mesh,
        in_specs=(P("inp", None, "chan"),),
        out_specs=P("inp", "chan", None, None),
        check_vma=False,
    )
```

```python
import functools
import math

import jax
import jax.numpy as jnp
import ml_dtypes
import numpy as np
from jax import lax
from jax.experimental import pallas as pl
from jax.experimental.pallas import tpu as pltpu
from jax.sharding import PartitionSpec as P

NCH = 512
NSPEC = 256
LANES = 128
ALL = ("inp", "chan")


def taper_weights(count):
    position = np.arange(count, dtype=np.float64)
    return 0.5 - 0.5 * np.cos(2.0 * np.pi * (position + 0.5) / count)


def by_lanes(table):
    table = table.reshape(*table.shape[:-1], -1, LANES)
    return np.moveaxis(table, -2, -3).astype(np.float32).astype(ml_dtypes.bfloat16)


def channel_tables():
    half = NCH // 2
    index = np.arange(NCH)
    angle = 2.0 * np.pi / NCH * (np.arange(half + 16)[:, None] * index[None, :] % NCH)
    window = taper_weights(NCH)[None, :] / math.sqrt(NCH)
    cosine = window * np.cos(angle)
    cosine[half + 1 :] = 0.0
    sine = (window * np.sin(angle))[:half]
    return tuple(by_lanes(part) for part in (cosine, sine))


def delay_tables():
    half = NCH // 2
    owner = np.arange(half)
    channel = np.stack([owner, np.where(owner == 0, half, NCH - owner)])
    angle = 2.0 * np.pi / NCH * (channel[:, :, None] * np.arange(half) % NCH)
    weight = taper_weights(NCH)[channel][:, :, None] * math.sqrt(NSPEC / NCH)
    cosine, sine = (
        table.reshape(2, half // 2, 2, half).transpose(2, 0, 1, 3).reshape(2, half, half)
        for table in (weight * np.cos(angle), weight * np.sin(angle))
    )
    upper = np.concatenate([cosine, -sine], axis=2)
    lower = np.concatenate([sine, cosine], axis=2)
    return by_lanes(np.concatenate([upper, lower], axis=1))


def joined(blocks):
    return jnp.concatenate([blocks[k] for k in range(blocks.shape[0])], axis=1)


def channelize_kernel(
    volt_hbm, cos_hbm, sin_hbm, out_ref, raw_ref, cos_ref, sin_ref, part_ref, wide_ref, sems, *, rows, specs
):
    half = NCH // 2
    tiles = NCH // LANES
    copies = [
        pltpu.make_async_copy(cos_hbm, cos_ref, sems.at[0]),
        pltpu.make_async_copy(sin_hbm, sin_ref, sems.at[1]),
    ]
    for spec in range(specs):
        copies.append(pltpu.make_async_copy(volt_hbm.at[:, spec], raw_ref.at[spec], sems.at[2 + spec]))
    for copy in (*copies[2:6], copies[0], copies[1], *copies[6:]):
        copy.start()

    def planes(spec):
        part_ref[spec] = raw_ref[spec].astype(jnp.float32).reshape(rows * 8, LANES)
        both = []
        for part in range(2):
            pieces = [part_ref[spec, pl.ds(2 * t + part, rows, stride=8), :] for t in range(tiles)]
            both.append(jnp.concatenate(pieces, axis=1).astype(jnp.bfloat16))
        return both

    contract = (((1,), (1,)), ((), ()))
    for pair in range(specs // 2):
        plain, turned = [], []
        if pair % 2 == 0:
            for copy in copies[2 + 2 * pair : 6 + 2 * pair]:
                copy.wait()
        for spec in (2 * pair, 2 * pair + 1):
            real, imag = planes(spec)
            plain += [real, imag]
            turned += [imag, -real]
        if pair == 0:
            copies[0].wait()
            copies[1].wait()
        even = lax.dot_general(
            joined(cos_ref), jnp.concatenate(plain, axis=0), contract, preferred_element_type=jnp.float32
        )
        odd = lax.dot_general(
            joined(sin_ref), jnp.concatenate(turned, axis=0), contract, preferred_element_type=jnp.float32
        )
        for k in range(2):
            spec = 2 * pair + k
            span = slice(k * LANES, (k + 1) * LANES)
            wide_ref[0, pl.ds(spec, half, stride=specs), :] = even[:half, span] + odd[:, span]
            wide_ref[1, pl.ds(spec, half, stride=specs), :] = even[:half, span] - odd[:, span]
            wide_ref[1, spec : spec + 1, :] = even[half : half + 1, span]
    first = wide_ref[0].reshape(half, specs, LANES)
    second = wide_ref[1].reshape(half, specs, LANES)
    out_ref[...] = jnp.concatenate([first, second], axis=1).astype(jnp.bfloat16)


def correlate_kernel(
    spec_ref, out_ref, left_ref, right_ref, row_ref, col_ref, stage_ref, sems, *, blocks, times, rows
):
    half = LANES // 2
    lane = lax.broadcasted_iota(jnp.int32, (1, LANES), 1)
    sign = jnp.where(lane < half, 1.0, -1.0)
    diagonal = lax.broadcasted_iota(jnp.int32, (rows, LANES), 1) % half == lax.broadcasted_iota(
        jnp.int32, (rows, LANES), 0
    )
    copies = []

    def prepare(ch, block):
        part = spec_ref[block * times : (block + 1) * times, ch * 8 : (ch + 1) * 8, :]
        wide = part.astype(jnp.float32).reshape(times * 8, LANES)
        narrow = wide.astype(jnp.bfloat16)
        right_ref[ch, block, :NSPEC] = narrow
        right_ref[ch, block, NSPEC:] = (pltpu.roll(wide, half, axis=1) * sign).astype(jnp.bfloat16)
        flipped = jnp.transpose(narrow)
        for part in range(2):
            for k in range(NSPEC // LANES):
                piece = flipped[part * rows : (part + 1) * rows, k * LANES : (k + 1) * LANES]
                left_ref[ch, part * (NSPEC // LANES) + k, block * rows : (block + 1) * rows] = piece
        total = jnp.sum(wide * wide, axis=0, keepdims=True)
        total = total + pltpu.roll(total, half, axis=1)
        scale = lax.rsqrt(total / NSPEC + 1e-06)
        col_ref[ch, block : block + 1, :] = scale

    def spread(ch):
        turned = jnp.transpose(col_ref[ch])[:rows] / NSPEC
        for block in range(blocks):
            column = jnp.broadcast_to(turned[:, block : block + 1], (rows, LANES))
            row_ref[ch, block * rows : (block + 1) * rows, :] = column

    def multiply(ch, pair):
        product = jnp.dot(
            joined(left_ref.at[ch]),
            joined(right_ref.at[ch, 2 * pair : 2 * pair + 2]),
            preferred_element_type=jnp.float32,
        )
        for iblock in (2 * pair, 2 * pair + 1):
            col = col_ref[ch, iblock : iblock + 1, :]
            for jblock in range(blocks):
                span = slice(jblock * rows, (jblock + 1) * rows)
                value = product[span, (iblock % 2) * LANES : (iblock % 2 + 1) * LANES]
                value = value * (row_ref[ch, span, :] * col)
                if iblock == jblock:
                    value = jnp.where(diagonal, 0.0, value)
                value = value.astype(jnp.bfloat16)
                for a in range(4):
                    stage_ref[ch, iblock, jblock, a] = value[a * 16 : (a + 1) * 16]
            copy = pltpu.make_async_copy(
                stage_ref.at[ch, iblock], out_ref.at[iblock, :, :, ch], sems.at[ch, iblock]
            )
            copy.start()
            copies.append(copy)

    for block in range(blocks):
        prepare(0, block)
    spread(0)
    for pair in range(blocks // 2):
        multiply(0, pair)
        prepare(1, 2 * pair)
        prepare(1, 2 * pair + 1)
    spread(1)
    for pair in range(blocks // 2):
        multiply(1, pair)
    for copy in copies:
        copy.wait()


def delay_kernel(rho_ref, table_ref, out_ref, wide_ref, stage_ref, sems, *, owners, rows, cols):
    sections = 2 * cols // 8
    flat_ref = stage_ref.reshape(cols * rows * 8, LANES)
    copies = []

    def widen(section):
        part = rho_ref[:, section * 8 : (section + 1) * 8, :].astype(jnp.float32)
        part = part.reshape(owners // 2, 2, 8, LANES)
        for parity in range(2):
            wide_ref[section, parity] = part[:, parity].reshape(owners * 4, LANES)

    def transform(first, group):
        parts = []
        for parity in range(2):
            left = []
            for col in range(first, first + group):
                pieces = []
                for ch in range(2):
                    row = ch * cols + col
                    pieces.append(wide_ref[row // 8, parity, pl.ds(row % 8, owners // 2, stride=8), :])
                turned = jnp.transpose(jnp.concatenate(pieces, axis=0).astype(jnp.bfloat16))
                left.append(jnp.concatenate([turned[:rows], turned[rows:]], axis=1))
            left = jnp.concatenate(left, axis=0)
            parts.append(jnp.dot(left, joined(table_ref.at[parity]), preferred_element_type=jnp.float32))
        for g in range(group):
            even, odd = (product[g * rows : (g + 1) * rows] for product in parts)
            for side, total in enumerate((even + odd, even - odd)):
                for k in range(NCH // LANES):
                    part, kb = k // 2, 2 * side + k % 2
                    start = (first + g) * rows * 8 + kb * 2 + part
                    flat_ref[pl.ds(start, rows, stride=8), :] = total[:, k * LANES : (k + 1) * LANES]
            copy = pltpu.make_async_copy(
                stage_ref.at[first + g], out_ref.at[:, first + g], sems.at[first + g]
            )
            copy.start()
            copies.append(copy)

    ready = 0
    for first, group in ((0, 8), (8, 4), (12, 4)):
        while ready < first + group:
            for ch in range(2):
                widen((ch * cols + ready) // 8)
            ready += 8
        transform(first, group)
    for copy in copies:
        copy.wait()


def fast(array):
    return pltpu.with_memory_space_constraint(array, pltpu.VMEM)


def shards(voltages):
    rows, _, local_time = voltages.shape
    chan_count = lax.axis_size("chan")
    inp_count = lax.axis_size("inp")
    owners = chan_count * inp_count
    spec_local = local_time // NCH
    cols = rows * inp_count // chan_count
    inputs = rows * inp_count
    cosine, sine = channel_tables()
    slab = 2 * spec_local
    tiles = NCH // LANES
    whole = pl.BlockSpec(memory_space=pltpu.VMEM)
    place = pl.BlockSpec(memory_space=pl.ANY)

    rowed = voltages.reshape(rows, 2, local_time // LANES, LANES).transpose(0, 2, 1, 3)
    rowed = rowed.reshape(rows, spec_local, 2 * tiles, LANES)
    spectra = pl.pallas_call(
        functools.partial(channelize_kernel, rows=rows, specs=spec_local),
        out_shape=pltpu.VMEM((owners, slab, LANES), jnp.bfloat16),
        in_specs=[place] * 3,
        out_specs=whole,
        scratch_shapes=[
            pltpu.VMEM((spec_local, rows, 2 * tiles, LANES), jnp.bfloat16),
            pltpu.VMEM(cosine.shape, jnp.bfloat16),
            pltpu.VMEM(sine.shape, jnp.bfloat16),
            pltpu.VMEM((spec_local, rows * 2 * tiles, LANES), jnp.float32),
            pltpu.VMEM((2, NCH // 2 * spec_local, LANES), jnp.float32),
            pltpu.SemaphoreType.DMA((2 + spec_local,)),
        ],
        name="channelize",
    )(rowed, jnp.asarray(cosine), jnp.asarray(sine))

    turned = lax.all_to_all(spectra, ALL, 0, 0, tiled=True)

    rho = pl.pallas_call(
        functools.partial(correlate_kernel, blocks=inp_count, times=chan_count, rows=rows),
        out_shape=jax.ShapeDtypeStruct((inp_count, inp_count, 4, 2, cols, LANES), jnp.bfloat16),
        in_specs=[whole],
        out_specs=place,
        scratch_shapes=[
            pltpu.VMEM((2, 2 * NSPEC // LANES, inputs, LANES), jnp.bfloat16),
            pltpu.VMEM((2, inp_count, 2 * NSPEC, LANES), jnp.bfloat16),
            pltpu.VMEM((2, inputs, LANES), jnp.float32),
            pltpu.VMEM((2, inp_count, LANES), jnp.float32),
            pltpu.VMEM((2, inp_count, inp_count, 4, cols, LANES), jnp.bfloat16),
            pltpu.SemaphoreType.DMA((2, inp_count)),
        ],
        name="correlate",
    )(fast(turned))

    rho = lax.all_to_all(rho.reshape(owners, 2 * cols, LANES), ALL, 0, 0, tiled=True)

    out = pl.pallas_call(
        functools.partial(delay_kernel, owners=owners, rows=rows, cols=cols),
        out_shape=jax.ShapeDtypeStruct((rows, cols, 8, LANES), jnp.float32),
        in_specs=[whole] * 2,
        out_specs=place,
        scratch_shapes=[
            pltpu.VMEM((2 * cols // 8, 2, owners * 4, LANES), jnp.float32),
            pltpu.VMEM((cols, rows, 8, LANES), jnp.float32),
            pltpu.SemaphoreType.DMA((cols,)),
        ],
        name="delay",
    )(fast(rho), fast(jnp.asarray(delay_tables())))
    out = out.reshape(rows, cols, NCH // LANES, 2, LANES).transpose(0, 1, 3, 2, 4)
    return out.reshape(rows, cols, 2, NCH)


def solution(mesh):
    return jax.shard_map(
        shards,
        mesh=mesh,
        in_specs=(P("inp", None, "chan"),),
        out_specs=P("inp", "chan", None, None),
        check_vma=False,
    )
```

```python
import functools
import math

import jax
import jax.numpy as jnp
import ml_dtypes
import numpy as np
from jax import lax
from jax.experimental import pallas as pl
from jax.experimental.pallas import tpu as pltpu
from jax.sharding import PartitionSpec as P

NCH = 512
NSPEC = 256
LANES = 128
ALL = ("inp", "chan")


def taper_weights(count):
    position = np.arange(count, dtype=np.float64)
    return 0.5 - 0.5 * np.cos(2.0 * np.pi * (position + 0.5) / count)


def by_lanes(table):
    table = table.reshape(*table.shape[:-1], -1, LANES)
    return np.moveaxis(table, -2, -3).astype(np.float32).astype(ml_dtypes.bfloat16)


def channel_tables():
    half = NCH // 2
    index = np.arange(NCH)
    angle = 2.0 * np.pi / NCH * (np.arange(half + 16)[:, None] * index[None, :] % NCH)
    window = taper_weights(NCH)[None, :] / math.sqrt(NCH)
    cosine = window * np.cos(angle)
    cosine[half + 1 :] = 0.0
    sine = (window * np.sin(angle))[:half]
    return tuple(by_lanes(part) for part in (cosine, sine))


def delay_tables():
    half = NCH // 2
    owner = np.arange(half)
    channel = np.stack([owner, np.where(owner == 0, half, NCH - owner)])
    angle = 2.0 * np.pi / NCH * (channel[:, :, None] * np.arange(half) % NCH)
    weight = taper_weights(NCH)[channel][:, :, None] * math.sqrt(NSPEC / NCH)
    cosine, sine = (
        table.reshape(2, half // 2, 2, half).transpose(2, 0, 1, 3).reshape(2, half, half)
        for table in (weight * np.cos(angle), weight * np.sin(angle))
    )
    upper = np.concatenate([cosine, -sine], axis=2)
    lower = np.concatenate([sine, cosine], axis=2)
    return by_lanes(np.concatenate([upper, lower], axis=1))


def joined(blocks):
    return jnp.concatenate([blocks[k] for k in range(blocks.shape[0])], axis=1)


def channelize_kernel(
    volt_hbm, cos_hbm, sin_hbm, out_ref, raw_ref, cos_ref, sin_ref, part_ref, wide_ref, sems, *, rows, specs
):
    half = NCH // 2
    tiles = NCH // LANES
    copies = [
        pltpu.make_async_copy(cos_hbm, cos_ref, sems.at[0]),
        pltpu.make_async_copy(sin_hbm, sin_ref, sems.at[1]),
    ]
    for spec in range(specs):
        copies.append(pltpu.make_async_copy(volt_hbm.at[:, spec], raw_ref.at[spec], sems.at[2 + spec]))
    for copy in (*copies[2:6], copies[0], copies[1], *copies[6:]):
        copy.start()

    def planes(spec):
        part_ref[spec] = raw_ref[spec].astype(jnp.float32).reshape(rows * 8, LANES)
        both = []
        for part in range(2):
            pieces = [part_ref[spec, pl.ds(2 * t + part, rows, stride=8), :] for t in range(tiles)]
            both.append(jnp.concatenate(pieces, axis=1).astype(jnp.bfloat16))
        return both

    contract = (((1,), (1,)), ((), ()))
    for pair in range(specs // 2):
        plain, turned = [], []
        if pair % 2 == 0:
            for copy in copies[2 + 2 * pair : 6 + 2 * pair]:
                copy.wait()
        for spec in (2 * pair, 2 * pair + 1):
            real, imag = planes(spec)
            plain += [real, imag]
            turned += [imag, -real]
        if pair == 0:
            copies[0].wait()
            copies[1].wait()
        even = lax.dot_general(
            joined(cos_ref), jnp.concatenate(plain, axis=0), contract, preferred_element_type=jnp.float32
        )
        odd = lax.dot_general(
            joined(sin_ref), jnp.concatenate(turned, axis=0), contract, preferred_element_type=jnp.float32
        )
        for k in range(2):
            spec = 2 * pair + k
            span = slice(k * LANES, (k + 1) * LANES)
            wide_ref[0, pl.ds(spec, half, stride=specs), :] = even[:half, span] + odd[:, span]
            wide_ref[1, pl.ds(spec, half, stride=specs), :] = even[:half, span] - odd[:, span]
            wide_ref[1, spec : spec + 1, :] = even[half : half + 1, span]
    first = wide_ref[0].reshape(half, specs, LANES)
    second = wide_ref[1].reshape(half, specs, LANES)
    out_ref[...] = jnp.concatenate([first, second], axis=1).astype(jnp.bfloat16)


def correlate_kernel(
    spec_ref, out_ref, left_ref, right_ref, row_ref, col_ref, *, blocks, times, rows
):
    half = LANES // 2
    lane = lax.broadcasted_iota(jnp.int32, (1, LANES), 1)
    sign = jnp.where(lane < half, 1.0, -1.0)
    diagonal = lax.broadcasted_iota(jnp.int32, (rows, LANES), 1) % half == lax.broadcasted_iota(
        jnp.int32, (rows, LANES), 0
    )

    def prepare(ch, block):
        part = spec_ref[block * times : (block + 1) * times, ch * 8 : (ch + 1) * 8, :]
        wide = part.astype(jnp.float32).reshape(times * 8, LANES)
        narrow = wide.astype(jnp.bfloat16)
        right_ref[ch, block, :NSPEC] = narrow
        right_ref[ch, block, NSPEC:] = (pltpu.roll(wide, half, axis=1) * sign).astype(jnp.bfloat16)
        flipped = jnp.transpose(narrow)
        for part in range(2):
            for k in range(NSPEC // LANES):
                piece = flipped[part * rows : (part + 1) * rows, k * LANES : (k + 1) * LANES]
                left_ref[ch, part * (NSPEC // LANES) + k, block * rows : (block + 1) * rows] = piece
        total = jnp.sum(wide * wide, axis=0, keepdims=True)
        total = total + pltpu.roll(total, half, axis=1)
        scale = lax.rsqrt(total / NSPEC + 1e-06)
        col_ref[ch, block : block + 1, :] = scale

    def spread(ch):
        turned = jnp.transpose(col_ref[ch])[:rows] / NSPEC
        for block in range(blocks):
            column = jnp.broadcast_to(turned[:, block : block + 1], (rows, LANES))
            row_ref[ch, block * rows : (block + 1) * rows, :] = column

    def multiply(ch, pair):
        product = jnp.dot(
            joined(left_ref.at[ch]),
            joined(right_ref.at[ch, 2 * pair : 2 * pair + 2]),
            preferred_element_type=jnp.float32,
        )
        for iblock in (2 * pair, 2 * pair + 1):
            col = col_ref[ch, iblock : iblock + 1, :]
            for jblock in range(blocks):
                span = slice(jblock * rows, (jblock + 1) * rows)
                value = product[span, (iblock % 2) * LANES : (iblock % 2 + 1) * LANES]
                value = value * (row_ref[ch, span, :] * col)
                if iblock == jblock:
                    value = jnp.where(diagonal, 0.0, value)
                value = value.astype(jnp.bfloat16)
                for a in range(4):
                    owner = (iblock * blocks + jblock) * 4 + a
                    out_ref[owner, ch * 16 : (ch + 1) * 16] = value[a * 16 : (a + 1) * 16]

    for block in range(blocks):
        prepare(0, block)
    spread(0)
    for pair in range(blocks // 2):
        multiply(0, pair)
        prepare(1, 2 * pair)
        prepare(1, 2 * pair + 1)
    spread(1)
    for pair in range(blocks // 2):
        multiply(1, pair)


def delay_kernel(
    rho_hbm, table_ref, out_ref, rho_ref, wide_ref, stage_ref, sems, arrive, *, owners, rows, cols
):
    sections = 2 * cols // 8
    flat_ref = stage_ref.reshape(cols * rows * 8, LANES)
    copies = []
    order = [ch * cols // 8 + k for k in range(cols // 8) for ch in range(2)]
    fetches = {
        k: pltpu.make_async_copy(rho_hbm.at[:, k * 8 : (k + 1) * 8], rho_ref.at[k], arrive.at[k]) for k in order
    }
    for k in order:
        fetches[k].start()

    def widen(section):
        part = rho_ref[section].astype(jnp.float32)
        part = part.reshape(owners // 2, 2, 8, LANES)
        for parity in range(2):
            wide_ref[section, parity] = part[:, parity].reshape(owners * 4, LANES)

    def transform(first, group):
        parts = []
        for parity in range(2):
            left = []
            for col in range(first, first + group):
                pieces = []
                for ch in range(2):
                    row = ch * cols + col
                    pieces.append(wide_ref[row // 8, parity, pl.ds(row % 8, owners // 2, stride=8), :])
                turned = jnp.transpose(jnp.concatenate(pieces, axis=0).astype(jnp.bfloat16))
                left.append(jnp.concatenate([turned[:rows], turned[rows:]], axis=1))
            left = jnp.concatenate(left, axis=0)
            parts.append(jnp.dot(left, joined(table_ref.at[parity]), preferred_element_type=jnp.float32))
        for g in range(group):
            even, odd = (product[g * rows : (g + 1) * rows] for product in parts)
            for side, total in enumerate((even + odd, even - odd)):
                for k in range(NCH // LANES):
                    part, kb = k // 2, 2 * side + k % 2
                    start = (first + g) * rows * 8 + kb * 2 + part
                    flat_ref[pl.ds(start, rows, stride=8), :] = total[:, k * LANES : (k + 1) * LANES]
            copy = pltpu.make_async_copy(
                stage_ref.at[first + g], out_ref.at[:, first + g], sems.at[first + g]
            )
            copy.start()
            copies.append(copy)

    ready = 0
    for first, group in ((0, 8), (8, 4), (12, 4)):
        while ready < first + group:
            both = [(ch * cols + ready) // 8 for ch in range(2)]
            for section in both:
                fetches[section].wait()
            for section in both:
                widen(section)
            ready += 8
        transform(first, group)
    for copy in copies:
        copy.wait()


def fast(array):
    return pltpu.with_memory_space_constraint(array, pltpu.VMEM)


def shards(voltages):
    rows, _, local_time = voltages.shape
    chan_count = lax.axis_size("chan")
    inp_count = lax.axis_size("inp")
    owners = chan_count * inp_count
    spec_local = local_time // NCH
    cols = rows * inp_count // chan_count
    inputs = rows * inp_count
    cosine, sine = channel_tables()
    slab = 2 * spec_local
    tiles = NCH // LANES
    whole = pl.BlockSpec(memory_space=pltpu.VMEM)
    place = pl.BlockSpec(memory_space=pl.ANY)

    rowed = voltages.reshape(rows, 2, local_time // LANES, LANES).transpose(0, 2, 1, 3)
    rowed = rowed.reshape(rows, spec_local, 2 * tiles, LANES)
    spectra = pl.pallas_call(
        functools.partial(channelize_kernel, rows=rows, specs=spec_local),
        out_shape=pltpu.VMEM((owners, slab, LANES), jnp.bfloat16),
        in_specs=[place] * 3,
        out_specs=whole,
        scratch_shapes=[
            pltpu.VMEM((spec_local, rows, 2 * tiles, LANES), jnp.bfloat16),
            pltpu.VMEM(cosine.shape, jnp.bfloat16),
            pltpu.VMEM(sine.shape, jnp.bfloat16),
            pltpu.VMEM((spec_local, rows * 2 * tiles, LANES), jnp.float32),
            pltpu.VMEM((2, NCH // 2 * spec_local, LANES), jnp.float32),
            pltpu.SemaphoreType.DMA((2 + spec_local,)),
        ],
        name="channelize",
    )(rowed, jnp.asarray(cosine), jnp.asarray(sine))

    turned = lax.all_to_all(spectra, ALL, 0, 0, tiled=True)

    rho = pl.pallas_call(
        functools.partial(correlate_kernel, blocks=inp_count, times=chan_count, rows=rows),
        out_shape=pltpu.VMEM((owners, 2 * cols, LANES), jnp.bfloat16),
        in_specs=[whole],
        out_specs=whole,
        scratch_shapes=[
            pltpu.VMEM((2, 2 * NSPEC // LANES, inputs, LANES), jnp.bfloat16),
            pltpu.VMEM((2, inp_count, 2 * NSPEC, LANES), jnp.bfloat16),
            pltpu.VMEM((2, inputs, LANES), jnp.float32),
            pltpu.VMEM((2, inp_count, LANES), jnp.float32),
        ],
        name="correlate",
    )(fast(turned))

    rho = lax.all_to_all(rho, ALL, 0, 0, tiled=True)

    out = pl.pallas_call(
        functools.partial(delay_kernel, owners=owners, rows=rows, cols=cols),
        out_shape=jax.ShapeDtypeStruct((rows, cols, 8, LANES), jnp.float32),
        in_specs=[place, whole],
        out_specs=place,
        scratch_shapes=[
            pltpu.VMEM((2 * cols // 8, owners, 8, LANES), jnp.bfloat16),
            pltpu.VMEM((2 * cols // 8, 2, owners * 4, LANES), jnp.float32),
            pltpu.VMEM((cols, rows, 8, LANES), jnp.float32),
            pltpu.SemaphoreType.DMA((cols,)),
            pltpu.SemaphoreType.DMA((2 * cols // 8,)),
        ],
        name="delay",
    )(rho, fast(jnp.asarray(delay_tables())))
    out = out.reshape(rows, cols, NCH // LANES, 2, LANES).transpose(0, 1, 3, 2, 4)
    return out.reshape(rows, cols, 2, NCH)


def solution(mesh):
    return jax.shard_map(
        shards,
        mesh=mesh,
        in_specs=(P("inp", None, "chan"),),
        out_specs=P("inp", "chan", None, None),
        check_vma=False,
    )
```

```python
import functools
import math

import jax
import jax.numpy as jnp
import ml_dtypes
import numpy as np
from jax import lax
from jax.experimental import pallas as pl
from jax.experimental.pallas import tpu as pltpu
from jax.sharding import PartitionSpec as P

NCH = 512
NSPEC = 256
LANES = 128
GROUPS = (4, 4, 4, 4)
ALL = ("inp", "chan")


def taper_weights(count):
    position = np.arange(count, dtype=np.float64)
    return 0.5 - 0.5 * np.cos(2.0 * np.pi * (position + 0.5) / count)


def by_lanes(table):
    table = table.reshape(*table.shape[:-1], -1, LANES)
    return np.moveaxis(table, -2, -3).astype(np.float32).astype(ml_dtypes.bfloat16)


def channel_tables():
    half = NCH // 2
    index = np.arange(NCH)
    angle = 2.0 * np.pi / NCH * (np.arange(half + 16)[:, None] * index[None, :] % NCH)
    window = taper_weights(NCH)[None, :] / math.sqrt(NCH)
    cosine = window * np.cos(angle)
    cosine[half + 1 :] = 0.0
    sine = (window * np.sin(angle))[:half]
    return tuple(by_lanes(part) for part in (cosine, sine))


def delay_tables():
    quarter = NCH // 4
    tables = []
    for kind in range(4):
        channel = []
        for ch, start in ((0, kind), (1, -kind % 4)):
            owner = np.arange(start, NCH // 2, 4)
            channel.append(owner if ch == 0 else np.where(owner == 0, NCH // 2, NCH - owner))
        channel = np.concatenate(channel)
        angle = 2.0 * np.pi / NCH * (channel[:, None] * np.arange(quarter) % NCH)
        weight = taper_weights(NCH)[channel][:, None] * math.sqrt(NSPEC / NCH)
        cosine, sine = weight * np.cos(angle), weight * np.sin(angle)
        tables.append(np.block([[cosine, -sine], [sine, cosine]]))
    return by_lanes(np.stack(tables))


def joined(blocks):
    return jnp.concatenate([blocks[k] for k in range(blocks.shape[0])], axis=1)


def channelize_kernel(
    volt_hbm, cos_hbm, sin_hbm, out_ref, raw_ref, cos_ref, sin_ref, part_ref, wide_ref, sems, *, rows, specs
):
    half = NCH // 2
    tiles = NCH // LANES
    copies = [
        pltpu.make_async_copy(cos_hbm, cos_ref, sems.at[0]),
        pltpu.make_async_copy(sin_hbm, sin_ref, sems.at[1]),
    ]
    for spec in range(specs):
        copies.append(pltpu.make_async_copy(volt_hbm.at[:, spec], raw_ref.at[spec], sems.at[2 + spec]))
    for copy in (*copies[2:4], copies[0], copies[1], *copies[4:]):
        copy.start()

    def planes(spec):
        part_ref[spec] = raw_ref[spec].astype(jnp.float32).reshape(rows * 8, LANES)
        both = []
        for part in range(2):
            pieces = [part_ref[spec, pl.ds(2 * t + part, rows, stride=8), :] for t in range(tiles)]
            both.append(jnp.concatenate(pieces, axis=1).astype(jnp.bfloat16))
        return both

    contract = (((1,), (1,)), ((), ()))
    for pair in range(specs // 2):
        plain, turned = [], []
        if pair < 2:
            for copy in copies[4:] if pair else copies[2:4]:
                copy.wait()
        for spec in (2 * pair, 2 * pair + 1):
            real, imag = planes(spec)
            plain += [real, imag]
            turned += [imag, -real]
        if pair == 0:
            copies[0].wait()
            copies[1].wait()
        even = lax.dot_general(
            joined(cos_ref), jnp.concatenate(plain, axis=0), contract, preferred_element_type=jnp.float32
        )
        odd = lax.dot_general(
            joined(sin_ref), jnp.concatenate(turned, axis=0), contract, preferred_element_type=jnp.float32
        )
        for k in range(2):
            spec = 2 * pair + k
            span = slice(k * LANES, (k + 1) * LANES)
            wide_ref[0, pl.ds(spec, half, stride=specs), :] = even[:half, span] + odd[:, span]
            wide_ref[1, pl.ds(spec, half, stride=specs), :] = even[:half, span] - odd[:, span]
            wide_ref[1, spec : spec + 1, :] = even[half : half + 1, span]
    first = wide_ref[0].reshape(half, specs, LANES)
    second = wide_ref[1].reshape(half, specs, LANES)
    out_ref[...] = jnp.concatenate([first, second], axis=1).astype(jnp.bfloat16)


def correlate_kernel(
    spec_ref, out_ref, left_ref, right_ref, row_ref, col_ref, stage_ref, sems, *, blocks, times, rows
):
    half = LANES // 2
    lane = lax.broadcasted_iota(jnp.int32, (1, LANES), 1)
    sign = jnp.where(lane < half, 1.0, -1.0)
    diagonal = lax.broadcasted_iota(jnp.int32, (rows, LANES), 1) % half == lax.broadcasted_iota(
        jnp.int32, (rows, LANES), 0
    )
    copies = []

    def prepare(ch, block):
        part = spec_ref[block * times : (block + 1) * times, ch * 8 : (ch + 1) * 8, :]
        wide = part.astype(jnp.float32).reshape(times * 8, LANES)
        narrow = wide.astype(jnp.bfloat16)
        right_ref[ch, block, :NSPEC] = narrow
        right_ref[ch, block, NSPEC:] = (pltpu.roll(wide, half, axis=1) * sign).astype(jnp.bfloat16)
        flipped = jnp.transpose(narrow)
        for part in range(2):
            for k in range(NSPEC // LANES):
                piece = flipped[part * rows : (part + 1) * rows, k * LANES : (k + 1) * LANES]
                left_ref[ch, part * (NSPEC // LANES) + k, block * rows : (block + 1) * rows] = piece
        total = jnp.sum(wide * wide, axis=0, keepdims=True)
        total = total + pltpu.roll(total, half, axis=1)
        scale = lax.rsqrt(total / NSPEC + 1e-06)
        col_ref[ch, block : block + 1, :] = scale

    def spread(ch):
        turned = jnp.transpose(col_ref[ch])[:rows] / NSPEC
        for block in range(blocks):
            column = jnp.broadcast_to(turned[:, block : block + 1], (rows, LANES))
            row_ref[ch, block * rows : (block + 1) * rows, :] = column

    def multiply(ch, pair):
        product = jnp.dot(
            joined(left_ref.at[ch]),
            joined(right_ref.at[ch, 2 * pair : 2 * pair + 2]),
            preferred_element_type=jnp.float32,
        )
        for iblock in (2 * pair, 2 * pair + 1):
            col = col_ref[ch, iblock : iblock + 1, :]
            for jblock in range(blocks):
                span = slice(jblock * rows, (jblock + 1) * rows)
                value = product[span, (iblock % 2) * LANES : (iblock % 2 + 1) * LANES]
                value = value * (row_ref[ch, span, :] * col)
                if iblock == jblock:
                    value = jnp.where(diagonal, 0.0, value)
                value = value.astype(jnp.bfloat16)
                for a in range(4):
                    stage_ref[ch, iblock, jblock, a] = value[a * 16 : (a + 1) * 16]
            copy = pltpu.make_async_copy(
                stage_ref.at[ch, iblock], out_ref.at[iblock, :, :, ch], sems.at[ch, iblock]
            )
            copy.start()
            copies.append(copy)

    for block in range(blocks):
        prepare(0, block)
    spread(0)
    for pair in range(blocks // 2):
        multiply(0, pair)
        prepare(1, 2 * pair)
        prepare(1, 2 * pair + 1)
    spread(1)
    for pair in range(blocks // 2):
        multiply(1, pair)
    for copy in copies:
        copy.wait()


def delay_kernel(rho_ref, table_ref, out_ref, wide_ref, stage_ref, sems, *, owners, rows, cols):
    sections = 2 * cols // 8
    flat_ref = stage_ref.reshape(cols * rows * 8, LANES)
    copies = []

    def widen(section):
        part = rho_ref[:, section * 8 : (section + 1) * 8, :].astype(jnp.float32)
        part = part.reshape(owners // 4, 4, 8, LANES)
        for kind in range(4):
            wide_ref[section, kind] = part[:, kind].reshape(owners * 2, LANES)

    def transform(first, group):
        parts = []
        for kind in range(4):
            left = []
            for col in range(first, first + group):
                pieces = []
                for ch, source in ((0, kind), (1, -kind % 4)):
                    row = ch * cols + col
                    pieces.append(wide_ref[row // 8, source, pl.ds(row % 8, owners // 4, stride=8), :])
                turned = jnp.transpose(jnp.concatenate(pieces, axis=0).astype(jnp.bfloat16))
                left.append(jnp.concatenate([turned[:rows], turned[rows:]], axis=1))
            left = jnp.concatenate(left, axis=0)
            parts.append(jnp.dot(left, joined(table_ref.at[kind]), preferred_element_type=jnp.float32))
        for g in range(group):
            zero, one, two, three = (
                (product[g * rows : (g + 1) * rows, :LANES], product[g * rows : (g + 1) * rows, LANES:])
                for product in parts
            )
            even, gap = [], []
            for part in range(2):
                even.append((zero[part] + two[part], one[part] + three[part]))
                gap.append((zero[part] - two[part], one[part] - three[part]))
            quarters = [
                (even[0][0] + even[0][1], even[1][0] + even[1][1]),
                (gap[0][0] + gap[1][1], gap[1][0] - gap[0][1]),
                (even[0][0] - even[0][1], even[1][0] - even[1][1]),
                (gap[0][0] - gap[1][1], gap[1][0] + gap[0][1]),
            ]
            for kb, pair in enumerate(quarters):
                for part in range(2):
                    start = (first + g) * rows * 8 + kb * 2 + part
                    flat_ref[pl.ds(start, rows, stride=8), :] = pair[part]
            copy = pltpu.make_async_copy(
                stage_ref.at[first + g], out_ref.at[:, first + g], sems.at[first + g]
            )
            copy.start()
            copies.append(copy)

    ready = first = 0
    for group in GROUPS:
        while ready < first + group:
            for ch in range(2):
                widen((ch * cols + ready) // 8)
            ready += 8
        transform(first, group)
        first += group
    for copy in copies:
        copy.wait()


def fast(array):
    return pltpu.with_memory_space_constraint(array, pltpu.VMEM)


def shards(voltages):
    rows, _, local_time = voltages.shape
    chan_count = lax.axis_size("chan")
    inp_count = lax.axis_size("inp")
    owners = chan_count * inp_count
    spec_local = local_time // NCH
    cols = rows * inp_count // chan_count
    inputs = rows * inp_count
    cosine, sine = channel_tables()
    slab = 2 * spec_local
    tiles = NCH // LANES
    whole = pl.BlockSpec(memory_space=pltpu.VMEM)
    place = pl.BlockSpec(memory_space=pl.ANY)

    rowed = voltages.reshape(rows, 2, local_time // LANES, LANES).transpose(0, 2, 1, 3)
    rowed = rowed.reshape(rows, spec_local, 2 * tiles, LANES)
    spectra = pl.pallas_call(
        functools.partial(channelize_kernel, rows=rows, specs=spec_local),
        out_shape=pltpu.VMEM((owners, slab, LANES), jnp.bfloat16),
        in_specs=[place] * 3,
        out_specs=whole,
        scratch_shapes=[
            pltpu.VMEM((spec_local, rows, 2 * tiles, LANES), jnp.bfloat16),
            pltpu.VMEM(cosine.shape, jnp.bfloat16),
            pltpu.VMEM(sine.shape, jnp.bfloat16),
            pltpu.VMEM((spec_local, rows * 2 * tiles, LANES), jnp.float32),
            pltpu.VMEM((2, NCH // 2 * spec_local, LANES), jnp.float32),
            pltpu.SemaphoreType.DMA((2 + spec_local,)),
        ],
        name="channelize",
    )(rowed, jnp.asarray(cosine), jnp.asarray(sine))

    turned = lax.all_to_all(spectra, ALL, 0, 0, tiled=True)

    rho = pl.pallas_call(
        functools.partial(correlate_kernel, blocks=inp_count, times=chan_count, rows=rows),
        out_shape=jax.ShapeDtypeStruct((inp_count, inp_count, 4, 2, cols, LANES), jnp.bfloat16),
        in_specs=[whole],
        out_specs=place,
        scratch_shapes=[
            pltpu.VMEM((2, 2 * NSPEC // LANES, inputs, LANES), jnp.bfloat16),
            pltpu.VMEM((2, inp_count, 2 * NSPEC, LANES), jnp.bfloat16),
            pltpu.VMEM((2, inputs, LANES), jnp.float32),
            pltpu.VMEM((2, inp_count, LANES), jnp.float32),
            pltpu.VMEM((2, inp_count, inp_count, 4, cols, LANES), jnp.bfloat16),
            pltpu.SemaphoreType.DMA((2, inp_count)),
        ],
        name="correlate",
    )(fast(turned))

    rho = lax.all_to_all(rho.reshape(owners, 2 * cols, LANES), ALL, 0, 0, tiled=True)

    out = pl.pallas_call(
        functools.partial(delay_kernel, owners=owners, rows=rows, cols=cols),
        out_shape=jax.ShapeDtypeStruct((rows, cols, 8, LANES), jnp.float32),
        in_specs=[whole] * 2,
        out_specs=place,
        scratch_shapes=[
            pltpu.VMEM((2 * cols // 8, 4, owners * 2, LANES), jnp.float32),
            pltpu.VMEM((cols, rows, 8, LANES), jnp.float32),
            pltpu.SemaphoreType.DMA((cols,)),
        ],
        name="delay",
    )(fast(rho), fast(jnp.asarray(delay_tables())))
    out = out.reshape(rows, cols, NCH // LANES, 2, LANES).transpose(0, 1, 3, 2, 4)
    return out.reshape(rows, cols, 2, NCH)


def solution(mesh):
    return jax.shard_map(
        shards,
        mesh=mesh,
        in_specs=(P("inp", None, "chan"),),
        out_specs=P("inp", "chan", None, None),
        check_vma=False,
    )
```

```python
import functools
import math

import jax
import jax.numpy as jnp
import ml_dtypes
import numpy as np
from jax import lax
from jax.experimental import pallas as pl
from jax.experimental.pallas import tpu as pltpu
from jax.sharding import PartitionSpec as P

NCH = 512
NSPEC = 256
LANES = 128
GROUPS = (8, 4, 2, 2)
ALL = ("inp", "chan")


def taper_weights(count):
    position = np.arange(count, dtype=np.float64)
    return 0.5 - 0.5 * np.cos(2.0 * np.pi * (position + 0.5) / count)


def by_lanes(table):
    table = table.reshape(*table.shape[:-1], -1, LANES)
    return np.moveaxis(table, -2, -3).astype(np.float32).astype(ml_dtypes.bfloat16)


def channel_tables():
    half = NCH // 2
    index = np.arange(NCH)
    angle = 2.0 * np.pi / NCH * (np.arange(half + 16)[:, None] * index[None, :] % NCH)
    window = taper_weights(NCH)[None, :] / math.sqrt(NCH)
    cosine = window * np.cos(angle)
    cosine[half + 1 :] = 0.0
    sine = (window * np.sin(angle))[:half]
    return tuple(by_lanes(part) for part in (cosine, sine))


def delay_tables():
    quarter = NCH // 4
    tables = []
    for kind in range(4):
        channel = []
        for ch, start in ((0, kind), (1, -kind % 4)):
            owner = np.arange(start, NCH // 2, 4)
            channel.append(owner if ch == 0 else np.where(owner == 0, NCH // 2, NCH - owner))
        channel = np.concatenate(channel)
        angle = 2.0 * np.pi / NCH * (channel[:, None] * np.arange(quarter) % NCH)
        weight = taper_weights(NCH)[channel][:, None] * math.sqrt(NSPEC / NCH)
        cosine, sine = weight * np.cos(angle), weight * np.sin(angle)
        tables.append(np.block([[cosine, -sine], [sine, cosine]]))
    return by_lanes(np.stack(tables))


def joined(blocks):
    return jnp.concatenate([blocks[k] for k in range(blocks.shape[0])], axis=1)


def channelize_kernel(
    volt_hbm, cos_hbm, sin_hbm, out_ref, raw_ref, cos_ref, sin_ref, part_ref, wide_ref, sems, *, rows, specs
):
    half = NCH // 2
    tiles = NCH // LANES
    copies = [
        pltpu.make_async_copy(cos_hbm, cos_ref, sems.at[0]),
        pltpu.make_async_copy(sin_hbm, sin_ref, sems.at[1]),
    ]
    for spec in range(specs):
        copies.append(pltpu.make_async_copy(volt_hbm.at[:, spec], raw_ref.at[spec], sems.at[2 + spec]))
    for copy in (*copies[2:4], copies[0], copies[1], *copies[4:]):
        copy.start()

    def planes(spec):
        part_ref[spec] = raw_ref[spec].astype(jnp.float32).reshape(rows * 8, LANES)
        both = []
        for part in range(2):
            pieces = [part_ref[spec, pl.ds(2 * t + part, rows, stride=8), :] for t in range(tiles)]
            both.append(jnp.concatenate(pieces, axis=1).astype(jnp.bfloat16))
        return both

    contract = (((1,), (1,)), ((), ()))
    for pair in range(specs // 2):
        plain, turned = [], []
        if pair < 2:
            for copy in copies[4:] if pair else copies[2:4]:
                copy.wait()
        for spec in (2 * pair, 2 * pair + 1):
            real, imag = planes(spec)
            plain += [real, imag]
            turned += [imag, -real]
        if pair == 0:
            copies[0].wait()
            copies[1].wait()
        even = lax.dot_general(
            joined(cos_ref), jnp.concatenate(plain, axis=0), contract, preferred_element_type=jnp.float32
        )
        odd = lax.dot_general(
            joined(sin_ref), jnp.concatenate(turned, axis=0), contract, preferred_element_type=jnp.float32
        )
        for k in range(2):
            spec = 2 * pair + k
            span = slice(k * LANES, (k + 1) * LANES)
            wide_ref[0, pl.ds(spec, half, stride=specs), :] = even[:half, span] + odd[:, span]
            wide_ref[1, pl.ds(spec, half, stride=specs), :] = even[:half, span] - odd[:, span]
            wide_ref[1, spec : spec + 1, :] = even[half : half + 1, span]
    first = wide_ref[0].reshape(half, specs, LANES)
    second = wide_ref[1].reshape(half, specs, LANES)
    out_ref[...] = jnp.concatenate([first, second], axis=1).astype(jnp.bfloat16)


def correlate_kernel(
    spec_ref, out_ref, left_ref, right_ref, row_ref, col_ref, stage_ref, sems, *, blocks, times, rows
):
    half = LANES // 2
    lane = lax.broadcasted_iota(jnp.int32, (1, LANES), 1)
    sign = jnp.where(lane < half, 1.0, -1.0)
    diagonal = lax.broadcasted_iota(jnp.int32, (rows, LANES), 1) % half == lax.broadcasted_iota(
        jnp.int32, (rows, LANES), 0
    )
    copies = []

    def prepare(ch, block):
        part = spec_ref[block * times : (block + 1) * times, ch * 8 : (ch + 1) * 8, :]
        wide = part.astype(jnp.float32).reshape(times * 8, LANES)
        narrow = wide.astype(jnp.bfloat16)
        right_ref[ch, block, :NSPEC] = narrow
        right_ref[ch, block, NSPEC:] = (pltpu.roll(wide, half, axis=1) * sign).astype(jnp.bfloat16)
        flipped = jnp.transpose(narrow)
        for part in range(2):
            for k in range(NSPEC // LANES):
                piece = flipped[part * rows : (part + 1) * rows, k * LANES : (k + 1) * LANES]
                left_ref[ch, part * (NSPEC // LANES) + k, block * rows : (block + 1) * rows] = piece
        total = jnp.sum(wide * wide, axis=0, keepdims=True)
        total = total + pltpu.roll(total, half, axis=1)
        scale = lax.rsqrt(total / NSPEC + 1e-06)
        col_ref[ch, block : block + 1, :] = scale

    def spread(ch):
        turned = jnp.transpose(col_ref[ch])[:rows] / NSPEC
        for block in range(blocks):
            column = jnp.broadcast_to(turned[:, block : block + 1], (rows, LANES))
            row_ref[ch, block * rows : (block + 1) * rows, :] = column

    def multiply(ch, pair):
        product = jnp.dot(
            joined(left_ref.at[ch]),
            joined(right_ref.at[ch, 2 * pair : 2 * pair + 2]),
            preferred_element_type=jnp.float32,
        )
        for iblock in (2 * pair, 2 * pair + 1):
            col = col_ref[ch, iblock : iblock + 1, :]
            for jblock in range(blocks):
                span = slice(jblock * rows, (jblock + 1) * rows)
                value = product[span, (iblock % 2) * LANES : (iblock % 2 + 1) * LANES]
                value = value * (row_ref[ch, span, :] * col)
                if iblock == jblock:
                    value = jnp.where(diagonal, 0.0, value)
                value = value.astype(jnp.bfloat16)
                for a in range(4):
                    stage_ref[ch, iblock, jblock, a] = value[a * 16 : (a + 1) * 16]
            copy = pltpu.make_async_copy(
                stage_ref.at[ch, iblock], out_ref.at[iblock, :, :, ch], sems.at[ch, iblock]
            )
            copy.start()
            copies.append(copy)

    for ch in range(2):
        for block in range(blocks):
            prepare(ch, block)
        spread(ch)
        for pair in range(blocks // 2):
            multiply(ch, pair)
    for copy in copies:
        copy.wait()


def delay_kernel(rho_ref, table_ref, out_ref, wide_ref, stage_ref, sems, *, owners, rows, cols):
    sections = 2 * cols // 8
    flat_ref = stage_ref.reshape(cols * rows * 8, LANES)
    copies = []

    def widen(section):
        part = rho_ref[:, section * 8 : (section + 1) * 8, :].astype(jnp.float32)
        part = part.reshape(owners // 4, 4, 8, LANES)
        for kind in range(4):
            wide_ref[section, kind] = part[:, kind].reshape(owners * 2, LANES)

    def transform(first, group):
        parts = []
        for kind in range(4):
            left = []
            for col in range(first, first + group):
                pieces = []
                for ch, source in ((0, kind), (1, -kind % 4)):
                    row = ch * cols + col
                    pieces.append(wide_ref[row // 8, source, pl.ds(row % 8, owners // 4, stride=8), :])
                turned = jnp.transpose(jnp.concatenate(pieces, axis=0).astype(jnp.bfloat16))
                left.append(jnp.concatenate([turned[:rows], turned[rows:]], axis=1))
            left = jnp.concatenate(left, axis=0)
            parts.append(jnp.dot(left, joined(table_ref.at[kind]), preferred_element_type=jnp.float32))
        for g in range(group):
            zero, one, two, three = (
                (product[g * rows : (g + 1) * rows, :LANES], product[g * rows : (g + 1) * rows, LANES:])
                for product in parts
            )
            even, gap = [], []
            for part in range(2):
                even.append((zero[part] + two[part], one[part] + three[part]))
                gap.append((zero[part] - two[part], one[part] - three[part]))
            quarters = [
                (even[0][0] + even[0][1], even[1][0] + even[1][1]),
                (gap[0][0] + gap[1][1], gap[1][0] - gap[0][1]),
                (even[0][0] - even[0][1], even[1][0] - even[1][1]),
                (gap[0][0] - gap[1][1], gap[1][0] + gap[0][1]),
            ]
            for kb, pair in enumerate(quarters):
                for part in range(2):
                    start = (first + g) * rows * 8 + kb * 2 + part
                    flat_ref[pl.ds(start, rows, stride=8), :] = pair[part]
            copy = pltpu.make_async_copy(
                stage_ref.at[first + g], out_ref.at[:, first + g], sems.at[first + g]
            )
            copy.start()
            copies.append(copy)

    ready = first = 0
    for group in GROUPS:
        while ready < first + group:
            for ch in range(2):
                widen((ch * cols + ready) // 8)
            ready += 8
        transform(first, group)
        first += group
    for copy in copies:
        copy.wait()


def fast(array):
    return pltpu.with_memory_space_constraint(array, pltpu.VMEM)


def shards(voltages):
    rows, _, local_time = voltages.shape
    chan_count = lax.axis_size("chan")
    inp_count = lax.axis_size("inp")
    owners = chan_count * inp_count
    spec_local = local_time // NCH
    cols = rows * inp_count // chan_count
    inputs = rows * inp_count
    cosine, sine = channel_tables()
    slab = 2 * spec_local
    tiles = NCH // LANES
    whole = pl.BlockSpec(memory_space=pltpu.VMEM)
    place = pl.BlockSpec(memory_space=pl.ANY)

    rowed = voltages.reshape(rows, 2, local_time // LANES, LANES).transpose(0, 2, 1, 3)
    rowed = rowed.reshape(rows, spec_local, 2 * tiles, LANES)
    spectra = pl.pallas_call(
        functools.partial(channelize_kernel, rows=rows, specs=spec_local),
        out_shape=pltpu.VMEM((owners, slab, LANES), jnp.bfloat16),
        in_specs=[place] * 3,
        out_specs=whole,
        scratch_shapes=[
            pltpu.VMEM((spec_local, rows, 2 * tiles, LANES), jnp.bfloat16),
            pltpu.VMEM(cosine.shape, jnp.bfloat16),
            pltpu.VMEM(sine.shape, jnp.bfloat16),
            pltpu.VMEM((spec_local, rows * 2 * tiles, LANES), jnp.float32),
            pltpu.VMEM((2, NCH // 2 * spec_local, LANES), jnp.float32),
            pltpu.SemaphoreType.DMA((2 + spec_local,)),
        ],
        name="channelize",
    )(rowed, jnp.asarray(cosine), jnp.asarray(sine))

    turned = lax.all_to_all(spectra, ALL, 0, 0, tiled=True)

    rho = pl.pallas_call(
        functools.partial(correlate_kernel, blocks=inp_count, times=chan_count, rows=rows),
        out_shape=jax.ShapeDtypeStruct((inp_count, inp_count, 4, 2, cols, LANES), jnp.bfloat16),
        in_specs=[whole],
        out_specs=place,
        scratch_shapes=[
            pltpu.VMEM((2, 2 * NSPEC // LANES, inputs, LANES), jnp.bfloat16),
            pltpu.VMEM((2, inp_count, 2 * NSPEC, LANES), jnp.bfloat16),
            pltpu.VMEM((2, inputs, LANES), jnp.float32),
            pltpu.VMEM((2, inp_count, LANES), jnp.float32),
            pltpu.VMEM((2, inp_count, inp_count, 4, cols, LANES), jnp.bfloat16),
            pltpu.SemaphoreType.DMA((2, inp_count)),
        ],
        name="correlate",
    )(fast(turned))

    rho = lax.all_to_all(rho.reshape(owners, 2 * cols, LANES), ALL, 0, 0, tiled=True)

    out = pl.pallas_call(
        functools.partial(delay_kernel, owners=owners, rows=rows, cols=cols),
        out_shape=jax.ShapeDtypeStruct((rows, cols, 8, LANES), jnp.float32),
        in_specs=[whole] * 2,
        out_specs=place,
        scratch_shapes=[
            pltpu.VMEM((2 * cols // 8, 4, owners * 2, LANES), jnp.float32),
            pltpu.VMEM((cols, rows, 8, LANES), jnp.float32),
            pltpu.SemaphoreType.DMA((cols,)),
        ],
        name="delay",
    )(fast(rho), fast(jnp.asarray(delay_tables())))
    out = out.reshape(rows, cols, NCH // LANES, 2, LANES).transpose(0, 1, 3, 2, 4)
    return out.reshape(rows, cols, 2, NCH)


def solution(mesh):
    return jax.shard_map(
        shards,
        mesh=mesh,
        in_specs=(P("inp", None, "chan"),),
        out_specs=P("inp", "chan", None, None),
        check_vma=False,
    )
```

```python
import functools
import math

import jax
import jax.numpy as jnp
import ml_dtypes
import numpy as np
from jax import lax
from jax.experimental import pallas as pl
from jax.experimental.pallas import tpu as pltpu
from jax.sharding import PartitionSpec as P

NCH = 512
NSPEC = 256
LANES = 128
GROUPS = (8, 4, 2, 2)
ALL = ("inp", "chan")


def taper_weights(count):
    position = np.arange(count, dtype=np.float64)
    return 0.5 - 0.5 * np.cos(2.0 * np.pi * (position + 0.5) / count)


def by_lanes(table):
    table = table.reshape(*table.shape[:-1], -1, LANES)
    return np.moveaxis(table, -2, -3).astype(np.float32).astype(ml_dtypes.bfloat16)


def channel_tables():
    half = NCH // 2
    index = np.arange(NCH)
    angle = 2.0 * np.pi / NCH * (np.arange(half + 16)[:, None] * index[None, :] % NCH)
    window = taper_weights(NCH)[None, :] / math.sqrt(NCH)
    cosine = window * np.cos(angle)
    cosine[half + 1 :] = 0.0
    sine = (window * np.sin(angle))[:half]
    return tuple(by_lanes(part) for part in (cosine, sine))


def delay_tables():
    quarter = NCH // 4
    tables = []
    for kind in range(4):
        channel = []
        for ch, start in ((0, kind), (1, -kind % 4)):
            owner = np.arange(start, NCH // 2, 4)
            channel.append(owner if ch == 0 else np.where(owner == 0, NCH // 2, NCH - owner))
        channel = np.concatenate(channel)
        angle = 2.0 * np.pi / NCH * (channel[:, None] * np.arange(quarter) % NCH)
        weight = taper_weights(NCH)[channel][:, None] * math.sqrt(NSPEC / NCH)
        cosine, sine = weight * np.cos(angle), weight * np.sin(angle)
        tables.append(np.block([[cosine, -sine], [sine, cosine]]))
    return by_lanes(np.stack(tables))


def joined(blocks):
    return jnp.concatenate([blocks[k] for k in range(blocks.shape[0])], axis=1)


def channelize_kernel(
    volt_hbm, cos_hbm, sin_hbm, out_ref, raw_ref, cos_ref, sin_ref, part_ref, wide_ref, sems, *, rows, specs
):
    half = NCH // 2
    tiles = NCH // LANES
    copies = [
        pltpu.make_async_copy(cos_hbm, cos_ref, sems.at[0]),
        pltpu.make_async_copy(sin_hbm, sin_ref, sems.at[1]),
    ]
    for spec in range(specs):
        copies.append(pltpu.make_async_copy(volt_hbm.at[:, spec], raw_ref.at[spec], sems.at[2 + spec]))
    for copy in (*copies[2:4], copies[0], copies[1], *copies[4:]):
        copy.start()

    def planes(spec):
        part_ref[spec] = raw_ref[spec].astype(jnp.float32).reshape(rows * 8, LANES)
        both = []
        for part in range(2):
            pieces = [part_ref[spec, pl.ds(2 * t + part, rows, stride=8), :] for t in range(tiles)]
            both.append(jnp.concatenate(pieces, axis=1).astype(jnp.bfloat16))
        return both

    contract = (((1,), (1,)), ((), ()))
    for pair in range(specs // 2):
        plain, turned = [], []
        if pair < 3:
            for copy in (copies[2:4], copies[4:6], copies[6:])[pair]:
                copy.wait()
        for spec in (2 * pair, 2 * pair + 1):
            real, imag = planes(spec)
            plain += [real, imag]
            turned += [imag, -real]
        if pair == 0:
            copies[0].wait()
            copies[1].wait()
        even = lax.dot_general(
            joined(cos_ref), jnp.concatenate(plain, axis=0), contract, preferred_element_type=jnp.float32
        )
        odd = lax.dot_general(
            joined(sin_ref), jnp.concatenate(turned, axis=0), contract, preferred_element_type=jnp.float32
        )
        for k in range(2):
            spec = 2 * pair + k
            span = slice(k * LANES, (k + 1) * LANES)
            wide_ref[0, pl.ds(spec, half, stride=specs), :] = even[:half, span] + odd[:, span]
            wide_ref[1, pl.ds(spec, half, stride=specs), :] = even[:half, span] - odd[:, span]
            wide_ref[1, spec : spec + 1, :] = even[half : half + 1, span]
    first = wide_ref[0].reshape(half, specs, LANES)
    second = wide_ref[1].reshape(half, specs, LANES)
    out_ref[...] = jnp.concatenate([first, second], axis=1).astype(jnp.bfloat16)


def correlate_kernel(
    spec_ref, out_ref, left_ref, right_ref, row_ref, col_ref, stage_ref, sems, *, blocks, times, rows
):
    half = LANES // 2
    lane = lax.broadcasted_iota(jnp.int32, (1, LANES), 1)
    sign = jnp.where(lane < half, 1.0, -1.0)
    diagonal = lax.broadcasted_iota(jnp.int32, (rows, LANES), 1) % half == lax.broadcasted_iota(
        jnp.int32, (rows, LANES), 0
    )
    copies = []

    def prepare(ch, block):
        part = spec_ref[block * times : (block + 1) * times, ch * 8 : (ch + 1) * 8, :]
        wide = part.astype(jnp.float32).reshape(times * 8, LANES)
        narrow = wide.astype(jnp.bfloat16)
        right_ref[ch, block, :NSPEC] = narrow
        right_ref[ch, block, NSPEC:] = (pltpu.roll(wide, half, axis=1) * sign).astype(jnp.bfloat16)
        flipped = jnp.transpose(narrow)
        for part in range(2):
            for k in range(NSPEC // LANES):
                piece = flipped[part * rows : (part + 1) * rows, k * LANES : (k + 1) * LANES]
                left_ref[ch, part * (NSPEC // LANES) + k, block * rows : (block + 1) * rows] = piece
        total = jnp.sum(wide * wide, axis=0, keepdims=True)
        total = total + pltpu.roll(total, half, axis=1)
        scale = lax.rsqrt(total / NSPEC + 1e-06)
        col_ref[ch, block : block + 1, :] = scale

    def spread(ch):
        turned = jnp.transpose(col_ref[ch])[:rows] / NSPEC
        for block in range(blocks):
            column = jnp.broadcast_to(turned[:, block : block + 1], (rows, LANES))
            row_ref[ch, block * rows : (block + 1) * rows, :] = column

    def multiply(ch, pair):
        product = jnp.dot(
            joined(left_ref.at[ch]),
            joined(right_ref.at[ch, 2 * pair : 2 * pair + 2]),
            preferred_element_type=jnp.float32,
        )
        for iblock in (2 * pair, 2 * pair + 1):
            col = col_ref[ch, iblock : iblock + 1, :]
            for jblock in range(blocks):
                span = slice(jblock * rows, (jblock + 1) * rows)
                value = product[span, (iblock % 2) * LANES : (iblock % 2 + 1) * LANES]
                value = value * (row_ref[ch, span, :] * col)
                if iblock == jblock:
                    value = jnp.where(diagonal, 0.0, value)
                value = value.astype(jnp.bfloat16)
                for a in range(4):
                    stage_ref[ch, iblock, jblock, a] = value[a * 16 : (a + 1) * 16]
            copy = pltpu.make_async_copy(
                stage_ref.at[ch, iblock], out_ref.at[iblock, :, :, ch], sems.at[ch, iblock]
            )
            copy.start()
            copies.append(copy)

    for ch in range(2):
        for block in range(blocks):
            prepare(ch, block)
        spread(ch)
        for pair in range(blocks // 2):
            multiply(ch, pair)
    for copy in copies:
        copy.wait()


def delay_kernel(rho_ref, table_ref, out_ref, wide_ref, stage_ref, sems, *, owners, rows, cols):
    sections = 2 * cols // 8
    flat_ref = stage_ref.reshape(cols * rows * 8, LANES)
    copies = []

    def widen(section):
        part = rho_ref[:, section * 8 : (section + 1) * 8, :].astype(jnp.float32)
        part = part.reshape(owners // 4, 4, 8, LANES)
        for kind in range(4):
            wide_ref[section, kind] = part[:, kind].reshape(owners * 2, LANES)

    def transform(first, group):
        parts = []
        for kind in range(4):
            left = []
            for col in range(first, first + group):
                pieces = []
                for ch, source in ((0, kind), (1, -kind % 4)):
                    row = ch * cols + col
                    pieces.append(wide_ref[row // 8, source, pl.ds(row % 8, owners // 4, stride=8), :])
                turned = jnp.transpose(jnp.concatenate(pieces, axis=0).astype(jnp.bfloat16))
                left.append(jnp.concatenate([turned[:rows], turned[rows:]], axis=1))
            left = jnp.concatenate(left, axis=0)
            parts.append(jnp.dot(left, joined(table_ref.at[kind]), preferred_element_type=jnp.float32))
        for g in range(group):
            zero, one, two, three = (
                (product[g * rows : (g + 1) * rows, :LANES], product[g * rows : (g + 1) * rows, LANES:])
                for product in parts
            )
            even, gap = [], []
            for part in range(2):
                even.append((zero[part] + two[part], one[part] + three[part]))
                gap.append((zero[part] - two[part], one[part] - three[part]))
            quarters = [
                (even[0][0] + even[0][1], even[1][0] + even[1][1]),
                (gap[0][0] + gap[1][1], gap[1][0] - gap[0][1]),
                (even[0][0] - even[0][1], even[1][0] - even[1][1]),
                (gap[0][0] - gap[1][1], gap[1][0] + gap[0][1]),
            ]
            for kb, pair in enumerate(quarters):
                for part in range(2):
                    start = (first + g) * rows * 8 + kb * 2 + part
                    flat_ref[pl.ds(start, rows, stride=8), :] = pair[part]
            copy = pltpu.make_async_copy(
                stage_ref.at[first + g], out_ref.at[:, first + g], sems.at[first + g]
            )
            copy.start()
            copies.append(copy)

    ready = first = 0
    for group in GROUPS:
        while ready < first + group:
            for ch in range(2):
                widen((ch * cols + ready) // 8)
            ready += 8
        transform(first, group)
        first += group
    for copy in copies:
        copy.wait()


def fast(array):
    return pltpu.with_memory_space_constraint(array, pltpu.VMEM)


def shards(voltages):
    rows, _, local_time = voltages.shape
    chan_count = lax.axis_size("chan")
    inp_count = lax.axis_size("inp")
    owners = chan_count * inp_count
    spec_local = local_time // NCH
    cols = rows * inp_count // chan_count
    inputs = rows * inp_count
    cosine, sine = channel_tables()
    slab = 2 * spec_local
    tiles = NCH // LANES
    whole = pl.BlockSpec(memory_space=pltpu.VMEM)
    place = pl.BlockSpec(memory_space=pl.ANY)

    rowed = voltages.reshape(rows, 2, local_time // LANES, LANES).transpose(0, 2, 1, 3)
    rowed = rowed.reshape(rows, spec_local, 2 * tiles, LANES)
    spectra = pl.pallas_call(
        functools.partial(channelize_kernel, rows=rows, specs=spec_local),
        out_shape=pltpu.VMEM((owners, slab, LANES), jnp.bfloat16),
        in_specs=[place] * 3,
        out_specs=whole,
        scratch_shapes=[
            pltpu.VMEM((spec_local, rows, 2 * tiles, LANES), jnp.bfloat16),
            pltpu.VMEM(cosine.shape, jnp.bfloat16),
            pltpu.VMEM(sine.shape, jnp.bfloat16),
            pltpu.VMEM((spec_local, rows * 2 * tiles, LANES), jnp.float32),
            pltpu.VMEM((2, NCH // 2 * spec_local, LANES), jnp.float32),
            pltpu.SemaphoreType.DMA((2 + spec_local,)),
        ],
        name="channelize",
    )(rowed, jnp.asarray(cosine), jnp.asarray(sine))

    turned = lax.all_to_all(spectra, ALL, 0, 0, tiled=True)

    rho = pl.pallas_call(
        functools.partial(correlate_kernel, blocks=inp_count, times=chan_count, rows=rows),
        out_shape=jax.ShapeDtypeStruct((inp_count, inp_count, 4, 2, cols, LANES), jnp.bfloat16),
        in_specs=[whole],
        out_specs=place,
        scratch_shapes=[
            pltpu.VMEM((2, 2 * NSPEC // LANES, inputs, LANES), jnp.bfloat16),
            pltpu.VMEM((2, inp_count, 2 * NSPEC, LANES), jnp.bfloat16),
            pltpu.VMEM((2, inputs, LANES), jnp.float32),
            pltpu.VMEM((2, inp_count, LANES), jnp.float32),
            pltpu.VMEM((2, inp_count, inp_count, 4, cols, LANES), jnp.bfloat16),
            pltpu.SemaphoreType.DMA((2, inp_count)),
        ],
        name="correlate",
    )(fast(turned))

    rho = lax.all_to_all(rho.reshape(owners, 2 * cols, LANES), ALL, 0, 0, tiled=True)

    out = pl.pallas_call(
        functools.partial(delay_kernel, owners=owners, rows=rows, cols=cols),
        out_shape=jax.ShapeDtypeStruct((rows, cols, 8, LANES), jnp.float32),
        in_specs=[whole] * 2,
        out_specs=place,
        scratch_shapes=[
            pltpu.VMEM((2 * cols // 8, 4, owners * 2, LANES), jnp.float32),
            pltpu.VMEM((cols, rows, 8, LANES), jnp.float32),
            pltpu.SemaphoreType.DMA((cols,)),
        ],
        name="delay",
    )(fast(rho), fast(jnp.asarray(delay_tables())))
    out = out.reshape(rows, cols, NCH // LANES, 2, LANES).transpose(0, 1, 3, 2, 4)
    return out.reshape(rows, cols, 2, NCH)


def solution(mesh):
    return jax.shard_map(
        shards,
        mesh=mesh,
        in_specs=(P("inp", None, "chan"),),
        out_specs=P("inp", "chan", None, None),
        check_vma=False,
    )
```
